512 devices in a mesh: dp: 64 (over z, y_hi, core), mp: 8 (over y_lo, x).
Axes of the slice: x: 4, y: 8 (y_hi: 4, y_lo: 2; y = y_hi * 2 + y_lo), z: 8, core: 2. Of those that a mesh axis runs over, the one named last changes fastest.
Arguments:
- views: bfloat16 [32768, 256], P('dp'), may hold values from -1 to 1
- partner: int32 [32768], P('dp'), may hold values from 0 to 32767, as said below
- weight: float32 [32768], P('dp'), may hold values from 0.25 to 4
Outputs:
- loss: float32 [32768], P('dp')
- grad: float32 [32768, 256], P('dp')
The draws below stay inside these ranges and needn't reach their ends.
Inputs may be any that keep to these rules, and one draw needn't show every extreme that they name: partner pairs the views: partner[partner[i]] = i and partner[i] != i.
All inputs are finite; a program needn't handle non-finite values.
Results may differ from the reference program's by a relative error of at most 0.0056.
Values may be sent and summed in bfloat16 or wider, within the bound.
No kernel may reach another device: no remote copies, remote signals or barrier semaphores. Data moves between devices by JAX's collectives and lax.ppermute only.
A program may use at most 64 MiB of HBM per device.

```python
import math
import jax
import jax.numpy as jnp
from jax import lax

W = 256
NV = 32768


def pairing(key):
    return jax.random.permutation(jax.random.fold_in(key, 7), NV).astype(jnp.int32)


def draw_partner(key, part):
    order = pairing(key)
    first = order[0::2]
    second = order[1::2]
    paired = jnp.zeros((NV,), jnp.int32)
    paired = paired.at[first].set(second)
    paired = paired.at[second].set(first)
    return paired


def noise_part(key, shape):
    return jax.random.truncated_normal(key, -4.0, 4.0, shape, jnp.float32)


def draw_views(key, part):
    order = pairing(key)
    image = jnp.zeros((NV,), jnp.int32).at[order].set(jnp.arange(NV, dtype=jnp.int32) // 2)
    groups = max(NV // 64, 4)
    images = NV // 2
    label = jax.random.randint(jax.random.fold_in(key, 11), (images,), 0, groups).astype(jnp.int32)
    tight = jax.random.uniform(jax.random.fold_in(key, 12), (groups,), jnp.float32, 0.1, 0.8)
    close = jax.random.uniform(jax.random.fold_in(key, 13), (images,), jnp.float32, 0.82, 0.95)
    view_label = label[image]
    class_share = tight[view_label]
    image_share = close[image] - class_share
    own_share = 1.0 - close[image]
    centres = noise_part(jax.random.fold_in(key, 21), (groups, W))
    image_dirs = noise_part(jax.random.fold_in(key, 22), (images, W))
    own = noise_part(jax.random.fold_in(key, 23), (NV, W))
    mixed = jnp.sqrt(class_share)[:, None] * centres[view_label]
    mixed = mixed + jnp.sqrt(image_share)[:, None] * image_dirs[image]
    mixed = mixed + jnp.sqrt(own_share)[:, None] * own
    common = noise_part(jax.random.fold_in(key, 24), (W,))
    loading = jax.random.uniform(jax.random.fold_in(key, 26), (NV,), jnp.float32, 0.0, 0.4)
    scale = jnp.exp(jax.random.uniform(jax.random.fold_in(key, 25), (NV,), jnp.float32, math.log(0.5), math.log(2.0)))
    mixed = jnp.sqrt(1.0 - loading)[:, None] * mixed + jnp.sqrt(loading)[:, None] * common[None, :]
    return jnp.clip(0.0625 * scale[:, None] * mixed, -1.0, 1.0).astype(jnp.bfloat16)


def shard_levels(key, dims, pieces, smallest, top_value):
    loudness, own = 1.0, jax.random.fold_in(key, 6)
    for dim, blocks in pieces:
        steps = jnp.exp(jax.random.uniform(jax.random.fold_in(own, dim), (blocks,), jnp.float32, smallest / len(pieces), top_value / len(pieces)))
        loudness = loudness * jnp.repeat(steps, dims[dim] // blocks).reshape([-1 if axis == dim else 1 for axis in range(len(dims))])
    return loudness


def setup_inputs(seed: int = 0) -> dict:
    streams_of = jax.random.split(jax.random.key(seed), 4)
    views = draw_views(jax.random.fold_in(streams_of[3], 71), 0)
    partner = draw_partner(jax.random.fold_in(streams_of[3], 71), 0)
    weight = jnp.clip(jnp.exp(math.log(4.0) - 2.7725887 * jax.random.uniform(streams_of[2], (NV,), jnp.float32) ** shard_levels(streams_of[2], (NV,), ((0, 64),), -0.2, 0.2)), 0.25, 4.0)
    return dict(views=views, partner=partner, weight=weight)


INV_TAU = 10.0
EPS = 1e-06

def reference(views, partner, weight):
    floats = views.astype(jnp.float32)
    length = jnp.sqrt(lax.optimization_barrier(jnp.sum(floats * floats, axis=1)) + EPS)
    unit = floats / length[:, None]
    normal = unit.astype(jnp.bfloat16)
    block = min(512, NV)
    count = NV // block
    col_ids = jnp.arange(NV, dtype=jnp.int32)

    def scores(index):
        start = (index * block).astype(jnp.int32)
        rows = lax.dynamic_slice_in_dim(normal, start, block, 0)
        s = jnp.dot(rows, normal.T, preferred_element_type=jnp.float32) * INV_TAU
        row_ids = start + jnp.arange(block, dtype=jnp.int32)
        mates = lax.dynamic_slice_in_dim(partner, start, block, 0)
        off = row_ids[:, None] != col_ids[None, :]
        match = mates[:, None] == col_ids[None, :]
        return (s, off, match, start)

    def first(index):
        s, off, match, start = scores(index)
        total = lax.optimization_barrier(jnp.sum(jnp.where(off, jnp.exp(s), jnp.float32(0.0)), axis=1))
        positive = lax.optimization_barrier(jnp.sum(jnp.where(match, s, jnp.float32(0.0)), axis=1))
        return (total, positive)
    total, positive = lax.map(first, jnp.arange(count, dtype=jnp.int32))
    lse = jnp.log(total.reshape(NV))
    loss = lse - positive.reshape(NV)

    def second(index):
        s, off, match, start = scores(index)
        lse_rows = lax.dynamic_slice_in_dim(lse, start, block, 0)
        w_rows = lax.dynamic_slice_in_dim(weight, start, block, 0)
        prow = jnp.exp(s - lse_rows[:, None])
        pcol = jnp.exp(s - lse[None, :])
        coef = jnp.where(off, w_rows[:, None] * prow + weight[None, :] * pcol, jnp.float32(0.0))
        coef = coef - jnp.where(match, w_rows[:, None] + weight[None, :], jnp.float32(0.0))
        coef = coef.astype(jnp.bfloat16)
        return jnp.dot(coef, normal, preferred_element_type=jnp.float32)
    g = lax.map(second, jnp.arange(count, dtype=jnp.int32)).reshape(NV, W) * INV_TAU
    grad = (g - unit * lax.optimization_barrier(jnp.sum(unit * g, axis=1, keepdims=True))) / length[:, None]
    return (loss, grad)
```

```python
import functools

import jax
import jax.numpy as jnp
from jax import lax
from jax.experimental import pallas as pl
from jax.experimental.pallas import tpu as pltpu
from jax.sharding import Mesh
from jax.sharding import PartitionSpec as P

INV_TAU = 10.0
EPS = 1e-06
LOG2E = 1.4426950408889634

DP = ("zh", "zl", "yh", "core")
MP = ("yl", "x")
FAR = ("yh", "zh")
TEAM = ("zl", "yl", "x")
OWNERS = ("core", "yh", "zh")

NT = (((1,), (1,)), ((), ()))


def swap(x, axis):
    return lax.ppermute(x, axis, [(0, 1), (1, 0)])


def exchange(x, axes):
    return lax.all_to_all(x, axes, 0, 0, tiled=True)


def scaled(x):
    floats = x.astype(jnp.float32)
    length = jnp.sqrt(jnp.sum(floats * floats, axis=1, keepdims=True) + EPS)
    return floats, length, 1.0 / length


def chunk_scalars(place, k, far_count, piece, sizes):
    zh, zl, yh, core, slot = (place[n] for n in range(5))
    q = k % far_count
    near = k >= far_count
    its_core = 1 - core if near else core
    its_yh, its_zh = q // sizes["zh"], q % sizes["zh"]
    group = ((its_zh * sizes["zl"] + zl) * sizes["yh"] + its_yh) * sizes["core"] + its_core
    base = (group * sizes["mp"] + slot) * piece
    if near:
        return base, None
    mine = jnp.logical_and(yh == its_yh, zh == its_zh)
    return base, jnp.where(mine, slot * piece, -(1 << 20))


def partner_ids(part_ref, oth_ref, rows):
    hi = oth_ref[pl.ds(rows, 8), :].astype(jnp.float32)
    ids = (hi[0:2] * 256.0 + hi[2:4]).astype(jnp.int32)
    other = jnp.concatenate([ids[n : n + 1] for n in range(ids.shape[0])], axis=1)
    return jnp.concatenate([part_ref[...], other], axis=1)


def forward_kernel(
    sizes, place, own, oth, far, near, part, weight, msg, ncol, nrow, s_buf
):
    rows, width = own.shape
    far_count, piece = far.shape[0], far.shape[1]
    half = far_count * piece
    block = 256
    for ref, source in ((0, own[...]), (rows, oth[0:rows, :])):
        floats, _, inverse = scaled(source)
        nrow[pl.ds(ref, rows), :] = (floats * inverse).astype(jnp.bfloat16)
    for at, ref in ((0, far), (half, near)):
        for q in range(far_count):
            floats, _, inverse = scaled(ref[q])
            ncol[pl.ds(at + q * piece, piece), :] = (floats * inverse).astype(jnp.bfloat16)

    both = 2 * rows
    step = 8
    ids = partner_ids(part, oth, rows)
    sub = lax.broadcasted_iota(jnp.int32, (step, both), 0)
    lane = lax.broadcasted_iota(jnp.int32, (step, rows), 1)
    mates = jnp.broadcast_to(ids, (step, both)) - sub
    diag = lane - sub[:, :rows]
    total = jnp.zeros((step, both), jnp.float32)
    positive = jnp.zeros((step, both), jnp.float32)
    right = nrow[...]
    for b in range(2 * half // block):
        s_buf[b % 2] = lax.dot_general(
            ncol[pl.ds(b * block, block), :], right, NT, preferred_element_type=jnp.float32
        )
        for c in range(block // piece):
            base, mine = chunk_scalars(place, b * (block // piece) + c, far_count, piece, sizes)
            for r in range(0, piece, step):
                s = s_buf[b % 2, pl.ds(c * piece + r, step), :]
                e = jnp.exp2(s * (INV_TAU * LOG2E))
                if mine is not None:
                    first = jnp.where(diag == mine + r, 0.0, e[:, :rows])
                    e = jnp.concatenate([first, e[:, rows:]], axis=1)
                total = total + e
                positive = jnp.where(mates == base + r, s, positive)
    total = jnp.sum(total, axis=0, keepdims=True)
    positive = jnp.sum(positive, axis=0, keepdims=True) * INV_TAU
    zl = place[1]
    same = [total[:, :rows], total[:, rows:], positive[:, :rows], weight[...]]
    turned = [total[:, rows:], total[:, :rows], positive[:, rows:], weight[...]]
    half_row = rows // 2

    def stacked(parts):
        return jnp.concatenate(
            [p[:, n * half_row : (n + 1) * half_row] for p in parts for n in range(2)], axis=0
        )

    same, turned = stacked(same), stacked(turned)
    members = sizes["mp"]
    for n in range(members):
        msg[zl * members + n] = same
        msg[(1 - zl) * members + n] = turned


def totals_kernel(sizes, place, got, weight, info, loss, cw):
    zl, slot = place[1], place[4]
    members = sizes["mp"]
    summed = got[0]
    for n in range(1, got.shape[0]):
        summed = summed + got[n]
    other_weight = got[(1 - zl) * members, 6:8, :]

    def joined(pair):
        return jnp.concatenate([pair[0:1], pair[1:2]], axis=1)

    total, total_other = joined(summed[0:2]), joined(summed[2:4])
    positive = joined(summed[4:6])
    other_weight = joined(other_weight)
    own_weight = weight[...]
    share = own_weight / total
    share_other = other_weight / total_other
    loss[...] = jnp.log(total) - positive
    info[...] = jnp.concatenate([share, share_other, own_weight, other_weight], axis=0)
    piece = own_weight.shape[1] // members
    out = jnp.zeros((1, 2 * piece), jnp.float32)
    for n in range(members):
        at = slice(n * piece, (n + 1) * piece)
        out = jnp.where(slot == n, jnp.concatenate([share[:, at], own_weight[:, at]], axis=1), out)
    for n in range(cw.shape[0]):
        cw[n] = out


def backward_kernel(
    sizes, place, own, oth, part, ncol, nrow, info, cw, msg, s_buf, coef, acc
):
    rows, width = own.shape
    owners = cw.shape[0]
    far_count = owners // 2
    half = ncol.shape[0] // 2
    piece = half // far_count
    block = 256
    both = 2 * rows
    step = 16
    core = place[3]
    shares = []
    for at in (core, 1 - core):
        flat = cw[pl.ds(at * far_count, far_count)].reshape(far_count, 2 * piece)
        shares.append(flat.T)
    ids = partner_ids(part, oth, rows)
    sub = lax.broadcasted_iota(jnp.int32, (step, both), 0)
    lane = lax.broadcasted_iota(jnp.int32, (step, rows), 1)
    mates = jnp.broadcast_to(ids, (step, both)) - sub
    diag = lane - sub[:, :rows]
    row_share = jnp.concatenate([info[0:1, :], info[1:2, :]], axis=1)
    row_weight = jnp.concatenate([info[2:3, :], info[3:4, :]], axis=1)
    row_share = jnp.broadcast_to(row_share, (step, both))
    row_weight = jnp.broadcast_to(row_weight, (step, both))
    right = nrow[...]
    for b in range(2 * half // block):
        s_buf[b % 2] = lax.dot_general(
            ncol[pl.ds(b * block, block), :], right, NT, preferred_element_type=jnp.float32
        )
        for c in range(block // piece):
            k = b * (block // piece) + c
            base, mine = chunk_scalars(place, k, far_count, piece, sizes)
            column = shares[k // far_count][:, k % far_count : k % far_count + 1]
            for r in range(0, piece, step):
                s = s_buf[b % 2, pl.ds(c * piece + r, step), :]
                e = jnp.exp2(s * (INV_TAU * LOG2E))
                if mine is not None:
                    first = jnp.where(diag == mine + r, 0.0, e[:, :rows])
                    e = jnp.concatenate([first, e[:, rows:]], axis=1)
                value = e * (row_share + column[r : r + step])
                pull = row_weight + column[piece + r : piece + r + step]
                value = jnp.where(mates == base + r, value - pull, value)
                coef[b % 2, pl.ds(c * piece + r, step), :] = value.astype(jnp.bfloat16)
        left = ncol[pl.ds(b * block, block), :].T
        product = jnp.dot(left, coef[b % 2], preferred_element_type=jnp.float32)
        if b == 0:
            acc[...] = product
        else:
            acc[...] += product
    zl = place[1]
    members = sizes["mp"]
    for at, first, source in ((zl, 0, own[...]), (1 - zl, rows, oth[0:rows, :])):
        floats, _, inverse = scaled(source)
        g = acc[:, first : first + rows].T * INV_TAU
        unit = floats * inverse
        out = (g - unit * jnp.sum(unit * g, axis=1, keepdims=True)) * inverse
        msg[pl.ds(at * members, members)] = out.astype(jnp.bfloat16).reshape(members, -1, width)


def shards(sizes, views, partner, weight):
    rows, width = views.shape
    members = sizes["mp"]
    piece = rows // members
    slot = lax.axis_index(MP)
    place = jnp.stack([lax.axis_index(a) for a in ("zh", "zl", "yh", "core")] + [slot])
    place = place.astype(jnp.int32)

    mine = lax.dynamic_slice_in_dim(views, slot * piece, piece, 0)
    packed = jnp.concatenate([partner >> 8, partner & 255]).astype(jnp.bfloat16)
    packed = packed.reshape(-1, width)
    packed = jnp.pad(packed, ((0, 16 - packed.shape[0]), (0, 0)))
    oth = swap(jnp.concatenate([views, packed], axis=0), "zl")
    far_count = sizes["zh"] * sizes["yh"]
    far = exchange(jnp.broadcast_to(mine[None], (far_count, piece, width)), FAR)
    near = swap(far, "core")

    part = partner.reshape(1, rows)
    heft = weight.reshape(1, rows)
    columns = 2 * far_count * piece
    smem = pl.BlockSpec(memory_space=pltpu.SMEM)
    vmem = pl.BlockSpec(memory_space=pltpu.VMEM)
    team = 2 * members
    f32, bf16 = jnp.float32, jnp.bfloat16
    params = pltpu.CompilerParams(vmem_limit_bytes=40 << 20)
    shape = jax.ShapeDtypeStruct
    flops = 2 * columns * 2 * rows * width
    msg, ncol, nrow = pl.pallas_call(
        functools.partial(forward_kernel, sizes),
        name="forward",
        in_specs=[smem] + [vmem] * 6,
        out_specs=[vmem] * 3,
        out_shape=[
            shape((team, 8, rows // 2), f32),
            shape((columns, width), bf16),
            shape((2 * rows, width), bf16),
        ],
        scratch_shapes=[pltpu.VMEM((2, 256, 2 * rows), f32)],
        compiler_params=params,
        cost_estimate=pl.CostEstimate(flops=flops, bytes_accessed=4 << 20, transcendentals=0),
    )(place, views, oth, far, near, part, heft)
    got = exchange(msg, TEAM)
    info, loss, cw = pl.pallas_call(
        functools.partial(totals_kernel, sizes),
        name="totals",
        in_specs=[smem] + [vmem] * 2,
        out_specs=[vmem] * 3,
        out_shape=[
            shape((4, rows), f32),
            shape((1, rows), f32),
            shape((2 * far_count, 1, 2 * piece), f32),
        ],
    )(place, got, heft)
    cw = exchange(cw, OWNERS)
    grads = pl.pallas_call(
        functools.partial(backward_kernel, sizes),
        name="backward",
        in_specs=[smem] + [vmem] * 7,
        out_specs=vmem,
        out_shape=shape((team, piece, width), bf16),
        scratch_shapes=[
            pltpu.VMEM((2, 256, 2 * rows), f32),
            pltpu.VMEM((2, 256, 2 * rows), bf16),
            pltpu.VMEM((width, 2 * rows), f32),
        ],
        compiler_params=params,
        cost_estimate=pl.CostEstimate(flops=2 * flops, bytes_accessed=4 << 20, transcendentals=0),
    )(place, views, oth, part, ncol, nrow, info, cw)
    shares = exchange(grads, TEAM)
    share = jnp.sum(shares.astype(f32), axis=0).astype(bf16)
    grad = exchange(jnp.broadcast_to(share[None], (members, piece, width)), MP)
    return loss.reshape(rows), grad.astype(f32).reshape(rows, width)


def solution(mesh):
    dims = {"zh": 4, "zl": 2, "yh": 4, "core": 2, "yl": 2, "x": 4}
    finer = Mesh(mesh.devices.reshape(tuple(dims.values())), tuple(dims))
    sizes = {**dims, "mp": dims["yl"] * dims["x"]}
    placed = (P(DP, None), P(DP), P(DP))
    return jax.shard_map(
        functools.partial(shards, sizes),
        mesh=finer,
        in_specs=placed,
        out_specs=(P(DP), P(DP, None)),
        check_vma=False,
    )
```

```python
import functools

import jax
import jax.numpy as jnp
from jax import lax
from jax.experimental import pallas as pl
from jax.experimental.pallas import tpu as pltpu
from jax.sharding import Mesh
from jax.sharding import PartitionSpec as P


INV_TAU = 10.0
EPS = 1e-06
LOG2E = 1.4426950408889634

DP = ("zh", "zl", "yh", "core")
MP = ("yl", "x")
FAR = ("yh", "zh")
TEAM = ("zl", "yl", "x")
OWNERS = ("core", "yh", "zh")

BLOCK = 256
NT = (((1,), (1,)), ((), ()))


def swap(x, axis):
    return lax.ppermute(x, axis, [(0, 1), (1, 0)])


def exchange(x, axes):
    return lax.all_to_all(x, axes, 0, 0, tiled=True)


def scaled(x):
    floats = x.astype(jnp.float32)
    length = jnp.sqrt(jnp.sum(floats * floats, axis=1, keepdims=True) + EPS)
    return floats, length, 1.0 / length


def place():
    zh, zl, yh, core = (lax.axis_index(a) for a in DP)
    return zh, zl, yh, core, lax.axis_index(MP)


def chunk_scalars(at, q, near, piece, sizes):
    zh, zl, yh, core, slot = at
    its_core = 1 - core if near else core
    its_yh, its_zh = q // sizes["zh"], q % sizes["zh"]
    group = ((its_zh * sizes["zl"] + zl) * sizes["yh"] + its_yh) * sizes["core"] + its_core
    base = (group * sizes["mp"] + slot) * piece
    if near:
        return base, None
    mine = jnp.logical_and(yh == its_yh, zh == its_zh)
    return base, jnp.where(mine, slot * piece, -(1 << 20))


def partner_ids(own_ref, oth_ref, rows):
    ids = []
    for ref in (own_ref, oth_ref):
        pair = ref[pl.ds(rows, 8), :].astype(jnp.float32)
        pair = (pair[0:2] * 256.0 + pair[2:4]).astype(jnp.int32)
        ids += [pair[n : n + 1] for n in range(pair.shape[0])]
    return jnp.concatenate(ids, axis=1)


def forward_half(sizes, at, near, source, ids, nrow, ncol, e_out, s_buf, total, positive):
    chunks, piece = source.shape[0], source.shape[1]
    both = nrow.shape[0]
    rows = both // 2
    for q in range(chunks):
        floats, _, inverse = scaled(source[q])
        ncol[pl.ds(q * piece, piece), :] = (floats * inverse).astype(jnp.bfloat16)
    step = 8
    sub = lax.broadcasted_iota(jnp.int32, (step, both), 0)
    mates = jnp.broadcast_to(ids, (step, both)) - sub
    if not near:
        diag = lax.broadcasted_iota(jnp.int32, (step, rows), 1) - sub[:, :rows]
    right = nrow[...]
    for b in range(chunks * piece // BLOCK):
        s_buf[b % 2] = lax.dot_general(
            ncol[pl.ds(b * BLOCK, BLOCK), :], right, NT, preferred_element_type=jnp.float32
        )
        for c in range(BLOCK // piece):
            base, mine = chunk_scalars(at, b * (BLOCK // piece) + c, near, piece, sizes)
            for r in range(0, piece, step):
                s = s_buf[b % 2, pl.ds(c * piece + r, step), :]
                e = jnp.exp2(s * (INV_TAU * LOG2E))
                if mine is not None:
                    first = jnp.where(diag == mine + r, 0.0, e[:, :rows])
                    e = jnp.concatenate([first, e[:, rows:]], axis=1)
                e_out[pl.ds(b * BLOCK + c * piece + r, step), :] = e
                total = total + e
                positive = jnp.where(mates == base + r, s, positive)
    return total, positive


def far_kernel(sizes, own, oth, far, sums, ncol, nrow, e_out, s_buf):
    rows = nrow.shape[0] // 2
    for at, source in ((0, own[0:rows, :]), (rows, oth[0:rows, :])):
        floats, _, inverse = scaled(source)
        nrow[pl.ds(at, rows), :] = (floats * inverse).astype(jnp.bfloat16)
    ids = partner_ids(own, oth, rows)
    zero = jnp.zeros((8, 2 * rows), jnp.float32)
    total, positive = forward_half(
        sizes, place(), False, far, ids, nrow, ncol, e_out, s_buf, zero, zero
    )
    sums[0] = total
    sums[1] = positive


def near_kernel(sizes, own, oth, near, weight, sums, nrow, msg, ncol, e_out, s_buf):
    rows = nrow.shape[0] // 2
    at = place()
    ids = partner_ids(own, oth, rows)
    total, positive = forward_half(
        sizes, at, True, near, ids, nrow, ncol, e_out, s_buf, sums[0], sums[1]
    )
    total = jnp.sum(total, axis=0, keepdims=True)
    positive = jnp.sum(positive, axis=0, keepdims=True) * INV_TAU
    zl = at[1]
    same = [total[:, :rows], total[:, rows:], positive[:, :rows], weight[...]]
    turned = [total[:, rows:], total[:, :rows], positive[:, rows:], weight[...]]
    half_row = rows // 2

    def stacked(parts):
        return jnp.concatenate(
            [p[:, n * half_row : (n + 1) * half_row] for p in parts for n in range(2)], axis=0
        )

    same, turned = stacked(same), stacked(turned)
    members = sizes["mp"]
    for n in range(members):
        msg[zl * members + n] = same
        msg[(1 - zl) * members + n] = turned


def totals_kernel(sizes, got, weight, info, loss, cw):
    _, zl, _, _, slot = place()
    members = sizes["mp"]
    summed = got[0]
    for n in range(1, got.shape[0]):
        summed = summed + got[n]
    other_weight = got[(1 - zl) * members, 6:8, :]

    def joined(pair):
        return jnp.concatenate([pair[0:1], pair[1:2]], axis=1)

    total, total_other = joined(summed[0:2]), joined(summed[2:4])
    positive = joined(summed[4:6])
    other_weight = joined(other_weight)
    own_weight = weight[...]
    share = own_weight / total
    share_other = other_weight / total_other
    loss[...] = jnp.log(total) - positive
    info[...] = jnp.concatenate([share, share_other, own_weight, other_weight], axis=0)
    piece = own_weight.shape[1] // members
    out = jnp.zeros((1, 2 * piece), jnp.float32)
    for n in range(members):
        at = slice(n * piece, (n + 1) * piece)
        out = jnp.where(slot == n, jnp.concatenate([share[:, at], own_weight[:, at]], axis=1), out)
    for n in range(cw.shape[0]):
        cw[n] = out


def backward_kernel(
    sizes, own, oth, ncol_far, ncol_near, e_far, e_near, info, cw, msg, coef, acc
):
    both, width = acc.shape[1], acc.shape[0]
    rows = both // 2
    chunks = cw.shape[0] // 2
    half = ncol_far.shape[0]
    piece = half // chunks
    step = 16
    at = place()
    ids = partner_ids(own, oth, rows)
    mates = jnp.broadcast_to(ids, (step, both)) - lax.broadcasted_iota(jnp.int32, (step, both), 0)
    row_share = jnp.concatenate([info[0:1, :], info[1:2, :]], axis=1)
    row_weight = jnp.concatenate([info[2:3, :], info[3:4, :]], axis=1)
    row_share = jnp.broadcast_to(row_share, (step, both))
    row_weight = jnp.broadcast_to(row_weight, (step, both))
    turn = 0
    for near, ncol, e_ref in ((False, ncol_far, e_far), (True, ncol_near, e_near)):
        core = 1 - at[3] if near else at[3]
        columns = cw[pl.ds(core * chunks, chunks)].reshape(chunks, 2 * piece).T
        for b in range(half // BLOCK):
            for c in range(BLOCK // piece):
                q = b * (BLOCK // piece) + c
                base, _ = chunk_scalars(at, q, near, piece, sizes)
                column = columns[:, q : q + 1]
                for r in range(0, piece, step):
                    e = e_ref[pl.ds(b * BLOCK + c * piece + r, step), :]
                    value = e * (row_share + column[r : r + step])
                    pull = row_weight + column[piece + r : piece + r + step]
                    value = jnp.where(mates == base + r, value - pull, value)
                    coef[turn % 2, pl.ds(c * piece + r, step), :] = value.astype(jnp.bfloat16)
            left = ncol[pl.ds(b * BLOCK, BLOCK), :].T
            product = jnp.dot(left, coef[turn % 2], preferred_element_type=jnp.float32)
            if turn == 0:
                acc[...] = product
            else:
                acc[...] += product
            turn += 1
    zl = at[1]
    members = sizes["mp"]
    for to, first, source in ((zl, 0, own[0:rows, :]), (1 - zl, rows, oth[0:rows, :])):
        floats, _, inverse = scaled(source)
        g = acc[:, first : first + rows].T * INV_TAU
        unit = floats * inverse
        out = (g - unit * jnp.sum(unit * g, axis=1, keepdims=True)) * inverse
        msg[pl.ds(to * members, members)] = out.astype(jnp.bfloat16).reshape(members, -1, width)


def call(kernel, outs, args, scratch=(), mib=4, flops=0):
    vmem = pl.BlockSpec(memory_space=pltpu.VMEM)
    return pl.pallas_call(
        kernel,
        in_specs=[vmem] * len(args),
        out_specs=[vmem] * len(outs),
        out_shape=[jax.ShapeDtypeStruct(*o) for o in outs],
        scratch_shapes=list(scratch),
        compiler_params=pltpu.CompilerParams(vmem_limit_bytes=mib << 20),
        cost_estimate=pl.CostEstimate(flops=flops, bytes_accessed=1 << 20, transcendentals=0),
    )(*args)


def shards(sizes, views, partner, weight):
    return body(sizes, views, partner, weight)


def body(sizes, views, partner, weight):
    rows, width = views.shape
    members = sizes["mp"]
    piece = rows // members
    slot = lax.axis_index(MP)
    f32, bf16 = jnp.float32, jnp.bfloat16

    packed = jnp.concatenate([partner >> 8, partner & 255]).astype(bf16).reshape(-1, width)
    packed = jnp.pad(packed, ((0, 16 - packed.shape[0]), (0, 0)))
    own = lax.optimization_barrier(jnp.concatenate([views, packed], axis=0))
    oth = swap(own, "zl")
    mine = lax.dynamic_slice_in_dim(own, slot * piece, piece, 0)
    chunks = sizes["zh"] * sizes["yh"]
    far = exchange(jnp.broadcast_to(mine[None], (chunks, piece, width)), FAR)
    near = swap(far, "core")

    heft = weight.reshape(1, rows)
    half, both, team = chunks * piece, 2 * rows, 2 * members
    flops = 2 * half * both * width
    score = pltpu.VMEM((2, BLOCK, both), f32)
    sums, ncol_far, nrow, e_far = call(
        functools.partial(far_kernel, sizes),
        [((2, 8, both), f32), ((half, width), bf16), ((both, width), bf16), ((half, both), f32)],
        (own, oth, far),
        [score],
        16,
        flops,
    )
    msg, ncol_near, e_near = call(
        functools.partial(near_kernel, sizes),
        [((team, 8, rows // 2), f32), ((half, width), bf16), ((half, both), f32)],
        (own, oth, near, heft, sums, nrow),
        [score],
        16,
        flops,
    )
    got = exchange(msg, TEAM)
    info, loss, cw = call(
        functools.partial(totals_kernel, sizes),
        [((4, rows), f32), ((1, rows), f32), ((2 * chunks, 1, 2 * piece), f32)],
        (got, heft),
    )
    cw = exchange(cw, OWNERS)
    (grads,) = call(
        functools.partial(backward_kernel, sizes),
        [((team, piece, width), bf16)],
        (own, oth, ncol_far, ncol_near, e_far, e_near, info, cw),
        [pltpu.VMEM((2, BLOCK, both), bf16), pltpu.VMEM((width, both), f32)],
        16,
        2 * flops,
    )
    shares = exchange(grads, TEAM)
    share = jnp.sum(shares.astype(f32), axis=0).astype(bf16)
    grad = exchange(jnp.broadcast_to(share[None], (members, piece, width)), MP)
    return loss.reshape(rows), grad.astype(f32).reshape(rows, width)


def solution(mesh):
    dims = {"zh": 4, "zl": 2, "yh": 4, "core": 2, "yl": 2, "x": 4}
    finer = Mesh(mesh.devices.reshape(tuple(dims.values())), tuple(dims))
    sizes = {**dims, "mp": dims["yl"] * dims["x"]}
    placed = (P(DP, None), P(DP), P(DP))
    return jax.shard_map(
        functools.partial(shards, sizes),
        mesh=finer,
        in_specs=placed,
        out_specs=(P(DP), P(DP, None)),
        check_vma=False,
    )
```

```python
import functools

import jax
import jax.numpy as jnp
from jax import lax
from jax.experimental import pallas as pl
from jax.experimental.pallas import tpu as pltpu
from jax.sharding import Mesh
from jax.sharding import PartitionSpec as P


INV_TAU = 10.0
EPS = 1e-06
LOG2E = 1.4426950408889634

DP = ("zh", "zl", "yh", "core")
MP = ("yl", "x")
FAR = ("yh", "zh")
TEAM = ("zl", "yl", "x")
OWNERS = ("core", "yh", "zh")

BLOCK = 256
NT = (((1,), (1,)), ((), ()))


def swap(x, axis):
    return lax.ppermute(x, axis, [(0, 1), (1, 0)])


def exchange(x, axes):
    return lax.all_to_all(x, axes, 0, 0, tiled=True)


def scaled(x):
    floats = x.astype(jnp.float32)
    length = jnp.sqrt(jnp.sum(floats * floats, axis=1, keepdims=True) + EPS)
    return floats, length, 1.0 / length


def place():
    zh, zl, yh, core = (lax.axis_index(a) for a in DP)
    return zh, zl, yh, core, lax.axis_index(MP)


def chunk_scalars(at, q, near, piece, sizes):
    zh, zl, yh, core, slot = at
    its_core = 1 - core if near else core
    its_yh, its_zh = q // sizes["zh"], q % sizes["zh"]
    group = ((its_zh * sizes["zl"] + zl) * sizes["yh"] + its_yh) * sizes["core"] + its_core
    base = (group * sizes["mp"] + slot) * piece
    if near:
        return base, None
    mine = jnp.logical_and(yh == its_yh, zh == its_zh)
    return base, jnp.where(mine, slot * piece, -(1 << 20))


def partner_ids(own_ref, oth_ref, rows):
    ids = []
    for ref in (own_ref, oth_ref):
        pair = ref[pl.ds(rows, 8), :].astype(jnp.float32)
        pair = (pair[0:2] * 256.0 + pair[2:4]).astype(jnp.int32)
        ids += [pair[n : n + 1] for n in range(pair.shape[0])]
    return jnp.concatenate(ids, axis=1)


def forward_half(sizes, at, near, source, ids, nrow, ncol, e_out, s_buf, total, positive):
    chunks, piece = source.shape[0], source.shape[1]
    both = nrow.shape[0]
    rows = both // 2
    for q in range(chunks):
        floats, _, inverse = scaled(source[q])
        ncol[pl.ds(q * piece, piece), :] = (floats * inverse).astype(jnp.bfloat16)
    step = 8
    sub = lax.broadcasted_iota(jnp.int32, (step, both), 0)
    mates = jnp.broadcast_to(ids, (step, both)) - sub
    if not near:
        diag = lax.broadcasted_iota(jnp.int32, (step, rows), 1) - sub[:, :rows]
    right = nrow[...]
    for b in range(chunks * piece // BLOCK):
        s_buf[b % 2] = lax.dot_general(
            ncol[pl.ds(b * BLOCK, BLOCK), :], right, NT, preferred_element_type=jnp.float32
        )
        for c in range(BLOCK // piece):
            base, mine = chunk_scalars(at, b * (BLOCK // piece) + c, near, piece, sizes)
            for r in range(0, piece, step):
                s = s_buf[b % 2, pl.ds(c * piece + r, step), :]
                e = jnp.exp2(s * (INV_TAU * LOG2E))
                if mine is not None:
                    first = jnp.where(diag == mine + r, 0.0, e[:, :rows])
                    e = jnp.concatenate([first, e[:, rows:]], axis=1)
                e_out[pl.ds(b * BLOCK + c * piece + r, step), :] = e
                total = total + e
                positive = jnp.where(mates == base + r, s, positive)
    return total, positive


def rows_kernel(own, oth, nrow, ids):
    rows = nrow.shape[0] // 2
    for at, source in ((0, own[0:rows, :]), (rows, oth[0:rows, :])):
        floats, _, inverse = scaled(source)
        nrow[pl.ds(at, rows), :] = (floats * inverse).astype(jnp.bfloat16)
    ids[...] = partner_ids(own, oth, rows)


def far_kernel(sizes, far, ids, nrow, sums, ncol, e_out, s_buf):
    zero = jnp.zeros((8, nrow.shape[0]), jnp.float32)
    total, positive = forward_half(
        sizes, place(), False, far, ids[...], nrow, ncol, e_out, s_buf, zero, zero
    )
    sums[0] = total
    sums[1] = positive


def near_kernel(sizes, near, ids, weight, sums, nrow, msg, ncol, e_out, s_buf):
    rows = nrow.shape[0] // 2
    at = place()
    total, positive = forward_half(
        sizes, at, True, near, ids[...], nrow, ncol, e_out, s_buf, sums[0], sums[1]
    )
    total = jnp.sum(total, axis=0, keepdims=True)
    positive = jnp.sum(positive, axis=0, keepdims=True) * INV_TAU
    zl = at[1]
    same = [total[:, :rows], total[:, rows:], positive[:, :rows], weight[...]]
    turned = [total[:, rows:], total[:, :rows], positive[:, rows:], weight[...]]
    half_row = rows // 2

    def stacked(parts):
        return jnp.concatenate(
            [p[:, n * half_row : (n + 1) * half_row] for p in parts for n in range(2)], axis=0
        )

    same, turned = stacked(same), stacked(turned)
    members = sizes["mp"]
    for n in range(members):
        msg[zl * members + n] = same
        msg[(1 - zl) * members + n] = turned


def totals_kernel(sizes, got, weight, info, loss, cw):
    _, zl, _, _, slot = place()
    members = sizes["mp"]
    summed = got[0]
    for n in range(1, got.shape[0]):
        summed = summed + got[n]
    other_weight = got[(1 - zl) * members, 6:8, :]

    def joined(pair):
        return jnp.concatenate([pair[0:1], pair[1:2]], axis=1)

    total, total_other = joined(summed[0:2]), joined(summed[2:4])
    positive = joined(summed[4:6])
    other_weight = joined(other_weight)
    own_weight = weight[...]
    share = own_weight / total
    share_other = other_weight / total_other
    loss[...] = jnp.log(total) - positive
    info[...] = jnp.concatenate([share, share_other, own_weight, other_weight], axis=0)
    piece = own_weight.shape[1] // members
    out = jnp.zeros((1, 2 * piece), jnp.float32)
    for n in range(members):
        at = slice(n * piece, (n + 1) * piece)
        out = jnp.where(slot == n, jnp.concatenate([share[:, at], own_weight[:, at]], axis=1), out)
    for n in range(cw.shape[0]):
        cw[n] = out


def backward_kernel(
    sizes, own, oth, ids, ncol_far, ncol_near, e_far, e_near, info, cw, msg, coef, acc
):
    both, width = acc.shape[1], acc.shape[0]
    rows = both // 2
    chunks = cw.shape[0] // 2
    half = ncol_far.shape[0]
    piece = half // chunks
    step = 16
    at = place()
    mates = jnp.broadcast_to(ids[...], (step, both)) - lax.broadcasted_iota(jnp.int32, (step, both), 0)
    row_share = jnp.concatenate([info[0:1, :], info[1:2, :]], axis=1)
    row_weight = jnp.concatenate([info[2:3, :], info[3:4, :]], axis=1)
    row_share = jnp.broadcast_to(row_share, (step, both))
    row_weight = jnp.broadcast_to(row_weight, (step, both))
    turn = 0
    for near, ncol, e_ref in ((False, ncol_far, e_far), (True, ncol_near, e_near)):
        core = 1 - at[3] if near else at[3]
        columns = cw[pl.ds(core * chunks, chunks)].reshape(chunks, 2 * piece).T
        for b in range(half // BLOCK):
            for c in range(BLOCK // piece):
                q = b * (BLOCK // piece) + c
                base, _ = chunk_scalars(at, q, near, piece, sizes)
                column = columns[:, q : q + 1]
                for r in range(0, piece, step):
                    e = e_ref[pl.ds(b * BLOCK + c * piece + r, step), :]
                    value = e * (row_share + column[r : r + step])
                    pull = row_weight + column[piece + r : piece + r + step]
                    value = jnp.where(mates == base + r, value - pull, value)
                    coef[turn % 2, pl.ds(c * piece + r, step), :] = value.astype(jnp.bfloat16)
            left = ncol[pl.ds(b * BLOCK, BLOCK), :].T
            product = jnp.dot(left, coef[turn % 2], preferred_element_type=jnp.float32)
            if turn == 0:
                acc[...] = product
            else:
                acc[...] += product
            turn += 1
    zl = at[1]
    members = sizes["mp"]
    for to, first, source in ((zl, 0, own[0:rows, :]), (1 - zl, rows, oth[0:rows, :])):
        floats, _, inverse = scaled(source)
        g = acc[:, first : first + rows].T * INV_TAU
        unit = floats * inverse
        out = (g - unit * jnp.sum(unit * g, axis=1, keepdims=True)) * inverse
        msg[pl.ds(to * members, members)] = out.astype(jnp.bfloat16).reshape(members, -1, width)


def call(kernel, outs, args, scratch=(), mib=4, flops=0):
    vmem = pl.BlockSpec(memory_space=pltpu.VMEM)
    return pl.pallas_call(
        kernel,
        in_specs=[vmem] * len(args),
        out_specs=[vmem] * len(outs),
        out_shape=[jax.ShapeDtypeStruct(*o) for o in outs],
        scratch_shapes=list(scratch),
        compiler_params=pltpu.CompilerParams(vmem_limit_bytes=mib << 20),
        cost_estimate=pl.CostEstimate(flops=flops, bytes_accessed=1 << 20, transcendentals=0),
    )(*args)


def shards(sizes, views, partner, weight):
    return body(sizes, views, partner, weight)


def body(sizes, views, partner, weight):
    rows, width = views.shape
    members = sizes["mp"]
    piece = rows // members
    slot = lax.axis_index(MP)
    f32, bf16 = jnp.float32, jnp.bfloat16

    mine = lax.dynamic_slice_in_dim(views, slot * piece, piece, 0)
    chunks = sizes["zh"] * sizes["yh"]
    far = exchange(jnp.broadcast_to(mine[None], (chunks, piece, width)), FAR)
    packed = jnp.concatenate([partner >> 8, partner & 255]).astype(bf16).reshape(-1, width)
    packed = jnp.pad(packed, ((0, 16 - packed.shape[0]), (0, 0)))
    own = lax.optimization_barrier(jnp.concatenate([views, packed], axis=0))
    oth = swap(own, "zl")
    both = 2 * rows
    nrow, ids = call(rows_kernel, [((both, width), bf16), ((1, both), jnp.int32)], (own, oth))
    near = swap(far, "core")

    heft = weight.reshape(1, rows)
    half, team = chunks * piece, 2 * members
    flops = 2 * half * both * width
    score = pltpu.VMEM((2, BLOCK, both), f32)
    sums, ncol_far, e_far = call(
        functools.partial(far_kernel, sizes),
        [((2, 8, both), f32), ((half, width), bf16), ((half, both), f32)],
        (far, ids, nrow),
        [score],
        16,
        flops,
    )
    msg, ncol_near, e_near = call(
        functools.partial(near_kernel, sizes),
        [((team, 8, rows // 2), f32), ((half, width), bf16), ((half, both), f32)],
        (near, ids, heft, sums, nrow),
        [score],
        16,
        flops,
    )
    got = exchange(msg, TEAM)
    info, loss, cw = call(
        functools.partial(totals_kernel, sizes),
        [((4, rows), f32), ((1, rows), f32), ((2 * chunks, 1, 2 * piece), f32)],
        (got, heft),
    )
    cw = exchange(cw, OWNERS)
    (grads,) = call(
        functools.partial(backward_kernel, sizes),
        [((team, piece, width), bf16)],
        (own, oth, ids, ncol_far, ncol_near, e_far, e_near, info, cw),
        [pltpu.VMEM((2, BLOCK, both), bf16), pltpu.VMEM((width, both), f32)],
        16,
        2 * flops,
    )
    shares = exchange(grads, TEAM)
    share = jnp.sum(shares.astype(f32), axis=0).astype(bf16)
    grad = exchange(jnp.broadcast_to(share[None], (members, piece, width)), MP)
    return loss.reshape(rows), grad.astype(f32).reshape(rows, width)


def solution(mesh):
    dims = {"zh": 4, "zl": 2, "yh": 4, "core": 2, "yl": 2, "x": 4}
    finer = Mesh(mesh.devices.reshape(tuple(dims.values())), tuple(dims))
    sizes = {**dims, "mp": dims["yl"] * dims["x"]}
    placed = (P(DP, None), P(DP), P(DP))
    return jax.shard_map(
        functools.partial(shards, sizes),
        mesh=finer,
        in_specs=placed,
        out_specs=(P(DP), P(DP, None)),
        check_vma=False,
    )
```

```python
import functools

import jax
import jax.numpy as jnp
from jax import lax
from jax.experimental import pallas as pl
from jax.experimental.pallas import tpu as pltpu
from jax.sharding import Mesh
from jax.sharding import PartitionSpec as P


INV_TAU = 10.0
EPS = 1e-06
LOG2E = 1.4426950408889634

DP = ("zh", "zl", "yh", "core")
MP = ("yl", "x")
FAR = ("yh", "zh")
TEAM = ("zl", "yl", "x")
OWNERS = ("core", "yh", "zh")

BLOCK = 256
NT = (((1,), (1,)), ((), ()))


def swap(x, axis):
    return lax.ppermute(x, axis, [(0, 1), (1, 0)])


def exchange(x, axes):
    return lax.all_to_all(x, axes, 0, 0, tiled=True)


def scaled(x):
    floats = x.astype(jnp.float32)
    length = jnp.sqrt(jnp.sum(floats * floats, axis=1, keepdims=True) + EPS)
    return floats, length, 1.0 / length


def place():
    zh, zl, yh, core = (lax.axis_index(a) for a in DP)
    return zh, zl, yh, core, lax.axis_index(MP)


def chunk_scalars(at, q, near, piece, sizes):
    zh, zl, yh, core, slot = at
    its_core = 1 - core if near else core
    its_yh, its_zh = q // sizes["zh"], q % sizes["zh"]
    group = ((its_zh * sizes["zl"] + zl) * sizes["yh"] + its_yh) * sizes["core"] + its_core
    base = (group * sizes["mp"] + slot) * piece
    if near:
        return base, None
    mine = jnp.logical_and(yh == its_yh, zh == its_zh)
    return base, jnp.where(mine, slot * piece, -(1 << 20))


def partner_ids(own_ref, oth_ref, rows):
    ids = []
    for ref in (own_ref, oth_ref):
        pair = ref[pl.ds(rows, 8), :].astype(jnp.float32)
        pair = (pair[0:2] * 256.0 + pair[2:4]).astype(jnp.int32)
        ids += [pair[n : n + 1] for n in range(pair.shape[0])]
    return jnp.concatenate(ids, axis=1)


def pack_kernel(views, part, weight, own, spread, heft, mates, arrived):
    rows = views.shape[0]
    piece = spread.shape[1]
    copy = pltpu.make_async_copy(views, own.at[pl.ds(0, rows)], arrived.at[0])
    small = pltpu.make_async_copy(part, mates, arrived.at[1])
    last = pltpu.make_async_copy(weight, heft, arrived.at[2])
    small.start()
    copy.start()
    last.start()
    small.wait()
    ids = mates[...]
    half_row = rows // 2
    parts = [x[:, n * half_row : (n + 1) * half_row] for x in (ids >> 8, ids & 255) for n in (0, 1)]
    blank = jnp.zeros((own.shape[0] - rows - 4, half_row), jnp.int32)
    packed = jnp.concatenate(parts + [blank], axis=0).astype(jnp.float32)
    own[pl.ds(rows, own.shape[0] - rows), :] = packed.astype(jnp.bfloat16)
    slot = lax.axis_index(MP)
    copy.wait()
    last.wait()
    mine = own[pl.ds(pl.multiple_of(slot * piece, piece), piece), :]
    for n in range(spread.shape[0]):
        spread[n] = mine


def forward_half(sizes, at, near, source, ids, nrow, ncol, e_out, s_buf, total, positive):
    chunks, piece = source.shape[0], source.shape[1]
    both = nrow.shape[0]
    rows = both // 2
    for q in range(chunks):
        floats, _, inverse = scaled(source[q])
        ncol[pl.ds(q * piece, piece), :] = (floats * inverse).astype(jnp.bfloat16)
    step = 8
    sub = lax.broadcasted_iota(jnp.int32, (step, both), 0)
    mates = jnp.broadcast_to(ids, (step, both)) - sub
    if not near:
        diag = lax.broadcasted_iota(jnp.int32, (step, rows), 1) - sub[:, :rows]
    right = nrow[...]
    for b in range(chunks * piece // BLOCK):
        s_buf[b % 2] = lax.dot_general(
            ncol[pl.ds(b * BLOCK, BLOCK), :], right, NT, preferred_element_type=jnp.float32
        )
        for c in range(BLOCK // piece):
            base, mine = chunk_scalars(at, b * (BLOCK // piece) + c, near, piece, sizes)
            for r in range(0, piece, step):
                s = s_buf[b % 2, pl.ds(c * piece + r, step), :]
                e = jnp.exp2(s * (INV_TAU * LOG2E))
                if mine is not None:
                    first = jnp.where(diag == mine + r, 0.0, e[:, :rows])
                    e = jnp.concatenate([first, e[:, rows:]], axis=1)
                e_out[pl.ds(b * BLOCK + c * piece + r, step), :] = e
                total = total + e
                positive = jnp.where(mates == base + r, s, positive)
    return total, positive


def far_kernel(sizes, own, oth, far, sums, ncol, nrow, e_out, s_buf):
    rows = nrow.shape[0] // 2
    for at, source in ((0, own[0:rows, :]), (rows, oth[0:rows, :])):
        floats, _, inverse = scaled(source)
        nrow[pl.ds(at, rows), :] = (floats * inverse).astype(jnp.bfloat16)
    ids = partner_ids(own, oth, rows)
    zero = jnp.zeros((8, 2 * rows), jnp.float32)
    total, positive = forward_half(
        sizes, place(), False, far, ids, nrow, ncol, e_out, s_buf, zero, zero
    )
    sums[0] = total
    sums[1] = positive


def near_kernel(sizes, own, oth, near, weight, sums, nrow, msg, ncol, e_out, s_buf):
    rows = nrow.shape[0] // 2
    at = place()
    ids = partner_ids(own, oth, rows)
    total, positive = forward_half(
        sizes, at, True, near, ids, nrow, ncol, e_out, s_buf, sums[0], sums[1]
    )
    total = jnp.sum(total, axis=0, keepdims=True)
    positive = jnp.sum(positive, axis=0, keepdims=True) * INV_TAU
    zl = at[1]
    same = [total[:, :rows], total[:, rows:], positive[:, :rows], weight[...]]
    turned = [total[:, rows:], total[:, :rows], positive[:, rows:], weight[...]]
    half_row = rows // 2

    def stacked(parts):
        return jnp.concatenate(
            [p[:, n * half_row : (n + 1) * half_row] for p in parts for n in range(2)], axis=0
        )

    same, turned = stacked(same), stacked(turned)
    members = sizes["mp"]
    for n in range(members):
        msg[zl * members + n] = same
        msg[(1 - zl) * members + n] = turned


def totals_kernel(sizes, got, weight, info, loss, cw):
    _, zl, _, _, slot = place()
    members = sizes["mp"]
    summed = got[0]
    for n in range(1, got.shape[0]):
        summed = summed + got[n]
    other_weight = got[(1 - zl) * members, 6:8, :]

    def joined(pair):
        return jnp.concatenate([pair[0:1], pair[1:2]], axis=1)

    total, total_other = joined(summed[0:2]), joined(summed[2:4])
    positive = joined(summed[4:6])
    other_weight = joined(other_weight)
    own_weight = weight[...]
    share = own_weight / total
    share_other = other_weight / total_other
    loss[...] = jnp.log(total) - positive
    info[...] = jnp.concatenate([share, share_other, own_weight, other_weight], axis=0)
    piece = own_weight.shape[1] // members
    out = jnp.zeros((1, 2 * piece), jnp.float32)
    for n in range(members):
        at = slice(n * piece, (n + 1) * piece)
        out = jnp.where(slot == n, jnp.concatenate([share[:, at], own_weight[:, at]], axis=1), out)
    for n in range(cw.shape[0]):
        cw[n] = out


def backward_kernel(
    sizes, own, oth, ncol_far, ncol_near, e_far, e_near, info, cw, msg, coef, acc
):
    both, width = acc.shape[1], acc.shape[0]
    rows = both // 2
    chunks = cw.shape[0] // 2
    half = ncol_far.shape[0]
    piece = half // chunks
    step = 16
    at = place()
    ids = partner_ids(own, oth, rows)
    mates = jnp.broadcast_to(ids, (step, both)) - lax.broadcasted_iota(jnp.int32, (step, both), 0)
    row_share = jnp.concatenate([info[0:1, :], info[1:2, :]], axis=1)
    row_weight = jnp.concatenate([info[2:3, :], info[3:4, :]], axis=1)
    row_share = jnp.broadcast_to(row_share, (step, both))
    row_weight = jnp.broadcast_to(row_weight, (step, both))
    turn = 0
    for near, ncol, e_ref in ((False, ncol_far, e_far), (True, ncol_near, e_near)):
        core = 1 - at[3] if near else at[3]
        columns = cw[pl.ds(core * chunks, chunks)].reshape(chunks, 2 * piece).T
        for b in range(half // BLOCK):
            for c in range(BLOCK // piece):
                q = b * (BLOCK // piece) + c
                base, _ = chunk_scalars(at, q, near, piece, sizes)
                column = columns[:, q : q + 1]
                for r in range(0, piece, step):
                    e = e_ref[pl.ds(b * BLOCK + c * piece + r, step), :]
                    value = e * (row_share + column[r : r + step])
                    pull = row_weight + column[piece + r : piece + r + step]
                    value = jnp.where(mates == base + r, value - pull, value)
                    coef[turn % 2, pl.ds(c * piece + r, step), :] = value.astype(jnp.bfloat16)
            left = ncol[pl.ds(b * BLOCK, BLOCK), :].T
            product = jnp.dot(left, coef[turn % 2], preferred_element_type=jnp.float32)
            if turn == 0:
                acc[...] = product
            else:
                acc[...] += product
            turn += 1
    zl = at[1]
    members = sizes["mp"]
    for to, first, source in ((zl, 0, own[0:rows, :]), (1 - zl, rows, oth[0:rows, :])):
        floats, _, inverse = scaled(source)
        g = acc[:, first : first + rows].T * INV_TAU
        unit = floats * inverse
        out = (g - unit * jnp.sum(unit * g, axis=1, keepdims=True)) * inverse
        msg[pl.ds(to * members, members)] = out.astype(jnp.bfloat16).reshape(members, -1, width)


def call(kernel, outs, args, scratch=(), mib=4, flops=0):
    vmem = pl.BlockSpec(memory_space=pltpu.VMEM)
    return pl.pallas_call(
        kernel,
        in_specs=[vmem] * len(args),
        out_specs=[vmem] * len(outs),
        out_shape=[jax.ShapeDtypeStruct(*o) for o in outs],
        scratch_shapes=list(scratch),
        compiler_params=pltpu.CompilerParams(vmem_limit_bytes=mib << 20),
        cost_estimate=pl.CostEstimate(flops=flops, bytes_accessed=1 << 20, transcendentals=0),
    )(*args)


def shards(sizes, views, partner, weight):
    return body(sizes, views, partner, weight)


def body(sizes, views, partner, weight):
    rows, width = views.shape
    members = sizes["mp"]
    piece = rows // members
    f32, bf16 = jnp.float32, jnp.bfloat16

    chunks = sizes["zh"] * sizes["yh"]
    own, spread, heft = pl.pallas_call(
        pack_kernel,
        name="pack",
        in_specs=[pl.BlockSpec(memory_space=pltpu.HBM)] * 3,
        out_specs=[pl.BlockSpec(memory_space=pltpu.VMEM)] * 3,
        out_shape=[
            jax.ShapeDtypeStruct((rows + 16, width), bf16),
            jax.ShapeDtypeStruct((chunks, piece, width), bf16),
            jax.ShapeDtypeStruct((1, rows), f32),
        ],
        scratch_shapes=[pltpu.VMEM((1, rows), jnp.int32), pltpu.SemaphoreType.DMA((3,))],
        compiler_params=pltpu.CompilerParams(vmem_limit_bytes=4 << 20),
    )(*[
        pltpu.with_memory_space_constraint(a, pltpu.HBM)
        for a in (views, partner.reshape(1, rows), weight.reshape(1, rows))
    ])
    oth = swap(own, "zl")
    far = exchange(spread, FAR)
    near = swap(far, "core")

    half, both, team = chunks * piece, 2 * rows, 2 * members
    flops = 2 * half * both * width
    score = pltpu.VMEM((2, BLOCK, both), f32)
    sums, ncol_far, nrow, e_far = call(
        functools.partial(far_kernel, sizes),
        [((2, 8, both), f32), ((half, width), bf16), ((both, width), bf16), ((half, both), f32)],
        (own, oth, far),
        [score],
        16,
        flops,
    )
    msg, ncol_near, e_near = call(
        functools.partial(near_kernel, sizes),
        [((team, 8, rows // 2), f32), ((half, width), bf16), ((half, both), f32)],
        (own, oth, near, heft, sums, nrow),
        [score],
        16,
        flops,
    )
    got = exchange(msg, TEAM)
    info, loss, cw = call(
        functools.partial(totals_kernel, sizes),
        [((4, rows), f32), ((1, rows), f32), ((2 * chunks, 1, 2 * piece), f32)],
        (got, heft),
    )
    cw = exchange(cw, OWNERS)
    (grads,) = call(
        functools.partial(backward_kernel, sizes),
        [((team, piece, width), bf16)],
        (own, oth, ncol_far, ncol_near, e_far, e_near, info, cw),
        [pltpu.VMEM((2, BLOCK, both), bf16), pltpu.VMEM((width, both), f32)],
        16,
        2 * flops,
    )
    shares = exchange(grads, TEAM)
    share = jnp.sum(shares.astype(f32), axis=0).astype(bf16)
    grad = exchange(jnp.broadcast_to(share[None], (members, piece, width)), MP)
    return loss.reshape(rows), grad.astype(f32).reshape(rows, width)


def solution(mesh):
    dims = {"zh": 4, "zl": 2, "yh": 4, "core": 2, "yl": 2, "x": 4}
    finer = Mesh(mesh.devices.reshape(tuple(dims.values())), tuple(dims))
    sizes = {**dims, "mp": dims["yl"] * dims["x"]}
    placed = (P(DP, None), P(DP), P(DP))
    return jax.shard_map(
        functools.partial(shards, sizes),
        mesh=finer,
        in_specs=placed,
        out_specs=(P(DP), P(DP, None)),
        check_vma=False,
    )
```

```python
import functools

import jax
import jax.numpy as jnp
from jax import lax
from jax.experimental import pallas as pl
from jax.experimental.pallas import tpu as pltpu
from jax.sharding import Mesh
from jax.sharding import PartitionSpec as P


INV_TAU = 10.0
EPS = 1e-06
LOG2E = 1.4426950408889634

DP = ("zh", "zl", "yh", "core")
MP = ("yl", "x")
FAR = ("yh", "zh")
TEAM = ("zl", "yl", "x")
OWNERS = ("core", "yh", "zh")

BLOCK = 256
NT = (((1,), (1,)), ((), ()))


def swap(x, axis):
    return lax.ppermute(x, axis, [(0, 1), (1, 0)])


def exchange(x, axes):
    return lax.all_to_all(x, axes, 0, 0, tiled=True)


def scaled(x):
    floats = x.astype(jnp.float32)
    length = jnp.sqrt(jnp.sum(floats * floats, axis=1, keepdims=True) + EPS)
    return floats, length, 1.0 / length


def place():
    zh, zl, yh, core = (lax.axis_index(a) for a in DP)
    return zh, zl, yh, core, lax.axis_index(MP)


def chunk_scalars(at, q, near, piece, sizes):
    zh, zl, yh, core, slot = at
    its_core = 1 - core if near else core
    its_yh, its_zh = q // sizes["zh"], q % sizes["zh"]
    group = ((its_zh * sizes["zl"] + zl) * sizes["yh"] + its_yh) * sizes["core"] + its_core
    base = (group * sizes["mp"] + slot) * piece
    if near:
        return base, None
    mine = jnp.logical_and(yh == its_yh, zh == its_zh)
    return base, jnp.where(mine, slot * piece, -(1 << 20))


def partner_ids(own_ref, oth_ref, rows):
    ids = []
    for ref in (own_ref, oth_ref):
        pair = ref[pl.ds(rows, 8), :].astype(jnp.float32)
        pair = (pair[0:2] * 256.0 + pair[2:4]).astype(jnp.int32)
        ids += [pair[n : n + 1] for n in range(pair.shape[0])]
    return jnp.concatenate(ids, axis=1)


def pack_kernel(views, part, weight, own, spread, heft, mates, arrived):
    rows = views.shape[0]
    piece = spread.shape[1]
    copy = pltpu.make_async_copy(views, own.at[pl.ds(0, rows)], arrived.at[0])
    small = pltpu.make_async_copy(part, mates, arrived.at[1])
    last = pltpu.make_async_copy(weight, heft, arrived.at[2])
    small.start()
    copy.start()
    last.start()
    small.wait()
    ids = mates[...]
    half_row = rows // 2
    parts = [x[:, n * half_row : (n + 1) * half_row] for x in (ids >> 8, ids & 255) for n in (0, 1)]
    blank = jnp.zeros((own.shape[0] - rows - 4, half_row), jnp.int32)
    packed = jnp.concatenate(parts + [blank], axis=0).astype(jnp.float32)
    own[pl.ds(rows, own.shape[0] - rows), :] = packed.astype(jnp.bfloat16)
    slot = lax.axis_index(MP)
    copy.wait()
    last.wait()
    mine = own[pl.ds(pl.multiple_of(slot * piece, piece), piece), :]
    for n in range(spread.shape[0]):
        spread[n] = mine


def forward_half(
    sizes, at, near, source, ids, nrow, ncol, s_buf, lanes, total, positive
):
    chunks, piece = source.shape[0], source.shape[1]
    both = nrow.shape[0]
    rows = both // 2
    for q in range(chunks):
        floats, _, inverse = scaled(source[q])
        ncol[pl.ds(q * piece, piece), :] = (floats * inverse).astype(jnp.bfloat16)
    step = 8
    sub = lax.broadcasted_iota(jnp.int32, (step, both), 0)
    mates = jnp.broadcast_to(ids, (step, both)) - sub
    if not near:
        diag = lax.broadcasted_iota(jnp.int32, (step, rows), 1) - sub[:, :rows]
    right = nrow[...]
    for b in range(chunks * piece // BLOCK):
        s_buf[b % 2] = lax.dot_general(
            ncol[pl.ds(b * BLOCK, BLOCK), :], right, NT, preferred_element_type=jnp.float32
        )
        for c in range(BLOCK // piece):
            base, mine = chunk_scalars(at, b * (BLOCK // piece) + c, near, piece, sizes)
            for r in range(0, piece, step):
                s = s_buf[b % 2, pl.ds(c * piece + r, step), :]
                e = jnp.exp2(s * (INV_TAU * LOG2E))
                if mine is not None:
                    first = jnp.where(diag == mine + r, 0.0, e[:, :rows])
                    e = jnp.concatenate([first, e[:, rows:]], axis=1)
                here = pl.ds(b * BLOCK + c * piece + r, step)
                across = e[:, :128]
                for n in range(128, both, 128):
                    across = across + e[:, n : n + 128]
                lanes[here, :] = across
                total = total + e
                positive = jnp.where(mates == base + r, s, positive)
    column = [
        jnp.sum(lanes[n : n + 128, :].T, axis=0, keepdims=True)
        for n in range(0, chunks * piece, 128)
    ]
    return total, positive, jnp.concatenate(column, axis=0)


def far_kernel(sizes, own, oth, far, sums, column, ncol, nrow, s_buf, lanes):
    rows = nrow.shape[0] // 2
    for at, source in ((0, own[0:rows, :]), (rows, oth[0:rows, :])):
        floats, _, inverse = scaled(source)
        nrow[pl.ds(at, rows), :] = (floats * inverse).astype(jnp.bfloat16)
    ids = partner_ids(own, oth, rows)
    zero = jnp.zeros((8, 2 * rows), jnp.float32)
    total, positive, column[...] = forward_half(
        sizes, place(), False, far, ids, nrow, ncol, s_buf, lanes, zero, zero
    )
    sums[0] = total
    sums[1] = positive


def near_kernel(
    sizes, own, oth, near, weight, sums, column, nrow, msg, cmsg, ncol, s_buf, lanes
):
    rows = nrow.shape[0] // 2
    at = place()
    ids = partner_ids(own, oth, rows)
    total, positive, last = forward_half(
        sizes, at, True, near, ids, nrow, ncol, s_buf, lanes, sums[0], sums[1]
    )
    members = sizes["mp"]
    piece = rows // members
    _, zl, _, core, slot = at
    mine = jnp.zeros((1, piece), jnp.float32)
    for n in range(members):
        mine = jnp.where(slot == n, weight[:, n * piece : (n + 1) * piece], mine)
    coarse = mine.astype(jnp.bfloat16).astype(jnp.float32)
    fine = jnp.concatenate([coarse, mine - coarse], axis=1)
    first = jnp.where(core == 0, column[...], last)
    second = jnp.where(core == 0, last, column[...])
    blank = jnp.zeros((7, 2 * piece), jnp.float32)
    packed = jnp.concatenate([first, second, fine, blank], axis=0).astype(jnp.bfloat16)
    for n in range(cmsg.shape[0]):
        cmsg[n] = packed

    total = jnp.sum(total, axis=0, keepdims=True)
    positive = jnp.sum(positive, axis=0, keepdims=True) * INV_TAU
    heft = jnp.where(slot == 0, weight[...], 0.0)
    none = jnp.zeros_like(heft)
    half_row = rows // 2
    for to, parts in (
        (zl, [total[:, :rows], positive[:, :rows], heft, none]),
        (1 - zl, [total[:, rows:], positive[:, rows:], none, none]),
    ):
        msg[to] = jnp.concatenate(
            [p[:, n * half_row : (n + 1) * half_row] for p in parts for n in range(2)], axis=0
        )


def totals_kernel(got, info, loss):
    zl = place()[1]

    def joined(group, n):
        return jnp.concatenate([group[n : n + 1], group[n + 1 : n + 2]], axis=1)

    own, other = got[zl], got[1 - zl]
    total, own_weight = joined(own, 0), joined(own, 4)
    other_weight = joined(other, 4)
    loss[...] = jnp.log(total) - joined(own, 2)
    info[...] = jnp.concatenate(
        [own_weight / total, other_weight / joined(other, 0), own_weight, other_weight], axis=0
    )


def backward_kernel(
    sizes, own, oth, nrow, ncol_far, ncol_near, info, cgot, msg, s_buf, coef, acc
):
    both, width = acc.shape[1], acc.shape[0]
    rows = both // 2
    chunks = cgot.shape[0] // 2
    half = ncol_far.shape[0]
    piece = half // chunks
    step = 16
    at = place()
    ids = partner_ids(own, oth, rows)
    sub = lax.broadcasted_iota(jnp.int32, (step, both), 0)
    mates = jnp.broadcast_to(ids, (step, both)) - sub
    diag = lax.broadcasted_iota(jnp.int32, (step, rows), 1) - sub[:, :rows]
    right = nrow[...]
    row_share = jnp.concatenate([info[0:1, :], info[1:2, :]], axis=1)
    row_weight = jnp.concatenate([info[2:3, :], info[3:4, :]], axis=1)
    row_share = jnp.broadcast_to(row_share, (step, both))
    row_weight = jnp.broadcast_to(row_weight, (step, both))
    column_total = cgot[0, 0:16, :].astype(jnp.float32)
    for n in range(1, 2 * chunks):
        column_total = column_total + cgot[n, 0:16, :].astype(jnp.float32)
    inverse_total = 1.0 / column_total
    turn = 0
    for near, ncol in ((False, ncol_far), (True, ncol_near)):
        core = 1 - at[3] if near else at[3]
        inverse = jnp.where(core == 0, inverse_total[0:8], inverse_total[8:16]).T
        heft = []
        for q in range(chunks):
            row = cgot[core * chunks + q, 16:24, :].astype(jnp.float32)[0:1]
            heft.append(row + jnp.concatenate([row[:, piece:], row[:, :piece]], axis=1))
        heft = jnp.concatenate(heft, axis=0).T
        for b in range(half // BLOCK):
            s_buf[turn % 2] = lax.dot_general(
                ncol[pl.ds(b * BLOCK, BLOCK), :], right, NT, preferred_element_type=jnp.float32
            )
            for c in range(BLOCK // piece):
                q = b * (BLOCK // piece) + c
                base, mine = chunk_scalars(at, q, near, piece, sizes)
                odd = slice(q % 2 * piece, (q % 2 + 1) * piece)
                pull_in = heft[odd, q : q + 1]
                column = pull_in * inverse[odd, q // 2 : q // 2 + 1]
                for r in range(0, piece, step):
                    s = s_buf[turn % 2, pl.ds(c * piece + r, step), :]
                    e = jnp.exp2(s * (INV_TAU * LOG2E))
                    if mine is not None:
                        first = jnp.where(diag == mine + r, 0.0, e[:, :rows])
                        e = jnp.concatenate([first, e[:, rows:]], axis=1)
                    value = e * (row_share + column[r : r + step])
                    pull = row_weight + pull_in[r : r + step]
                    value = jnp.where(mates == base + r, value - pull, value)
                    coef[turn % 2, pl.ds(c * piece + r, step), :] = value.astype(jnp.bfloat16)
            left = ncol[pl.ds(b * BLOCK, BLOCK), :].T
            product = jnp.dot(left, coef[turn % 2], preferred_element_type=jnp.float32)
            if turn == 0:
                acc[...] = product
            else:
                acc[...] += product
            turn += 1
    zl = at[1]
    members = sizes["mp"]
    for to, first, source in ((zl, 0, own[0:rows, :]), (1 - zl, rows, oth[0:rows, :])):
        floats, _, inverse = scaled(source)
        g = acc[:, first : first + rows].T * INV_TAU
        unit = floats * inverse
        out = (g - unit * jnp.sum(unit * g, axis=1, keepdims=True)) * inverse
        msg[pl.ds(to * members, members)] = out.astype(jnp.bfloat16).reshape(members, -1, width)


def call(kernel, outs, args, scratch=(), mib=4, flops=0):
    vmem = pl.BlockSpec(memory_space=pltpu.VMEM)
    return pl.pallas_call(
        kernel,
        in_specs=[vmem] * len(args),
        out_specs=[vmem] * len(outs),
        out_shape=[jax.ShapeDtypeStruct(*o) for o in outs],
        scratch_shapes=list(scratch),
        compiler_params=pltpu.CompilerParams(vmem_limit_bytes=mib << 20),
        cost_estimate=pl.CostEstimate(flops=flops, bytes_accessed=1 << 20, transcendentals=0),
    )(*args)


def shards(sizes, views, partner, weight):
    return body(sizes, views, partner, weight)


def body(sizes, views, partner, weight):
    rows, width = views.shape
    members = sizes["mp"]
    piece = rows // members
    f32, bf16 = jnp.float32, jnp.bfloat16

    chunks = sizes["zh"] * sizes["yh"]
    own, spread, heft = pl.pallas_call(
        pack_kernel,
        name="pack",
        in_specs=[pl.BlockSpec(memory_space=pltpu.HBM)] * 3,
        out_specs=[pl.BlockSpec(memory_space=pltpu.VMEM)] * 3,
        out_shape=[
            jax.ShapeDtypeStruct((rows + 16, width), bf16),
            jax.ShapeDtypeStruct((chunks, piece, width), bf16),
            jax.ShapeDtypeStruct((1, rows), f32),
        ],
        scratch_shapes=[pltpu.VMEM((1, rows), jnp.int32), pltpu.SemaphoreType.DMA((3,))],
        compiler_params=pltpu.CompilerParams(vmem_limit_bytes=4 << 20),
    )(*[
        pltpu.with_memory_space_constraint(a, pltpu.HBM)
        for a in (views, partner.reshape(1, rows), weight.reshape(1, rows))
    ])
    oth = swap(own, "zl")
    far = exchange(spread, FAR)
    near = swap(far, "core")

    half, both, team = chunks * piece, 2 * rows, 2 * members
    flops = 2 * half * both * width
    scratch = [pltpu.VMEM((2, BLOCK, both), f32), pltpu.VMEM((half, 128), f32)]
    sums, column, ncol_far, nrow = call(
        functools.partial(far_kernel, sizes),
        [
            ((2, 8, both), f32),
            ((half // 128, 128), f32),
            ((half, width), bf16),
            ((both, width), bf16),
        ],
        (own, oth, far),
        scratch,
        16,
        flops,
    )
    msg, cmsg, ncol_near = call(
        functools.partial(near_kernel, sizes),
        [
            ((2, 8, rows // 2), f32),
            ((2 * chunks, 24, 128), bf16),
            ((half, width), bf16),
        ],
        (own, oth, near, heft, sums, column, nrow),
        scratch,
        16,
        flops,
    )
    got = msg + swap(msg, "zl")
    cgot = exchange(cmsg, OWNERS)
    got = got + swap(got, "yl")
    for apart in (1, 2):
        got = got + lax.ppermute(got, "x", [(n, n ^ apart) for n in range(sizes["x"])])
    info, loss = call(totals_kernel, [((4, rows), f32), ((1, rows), f32)], (got,))
    (grads,) = call(
        functools.partial(backward_kernel, sizes),
        [((team, piece, width), bf16)],
        (own, oth, nrow, ncol_far, ncol_near, info, cgot),
        [pltpu.VMEM((2, BLOCK, both), f32), pltpu.VMEM((2, BLOCK, both), bf16), pltpu.VMEM((width, both), f32)],
        16,
        2 * flops,
    )
    shares = exchange(grads, TEAM)
    share = jnp.sum(shares.astype(f32), axis=0).astype(bf16)
    grad = exchange(jnp.broadcast_to(share[None], (members, piece, width)), MP)
    return loss.reshape(rows), grad.astype(f32).reshape(rows, width)


def solution(mesh):
    dims = {"zh": 4, "zl": 2, "yh": 4, "core": 2, "yl": 2, "x": 4}
    finer = Mesh(mesh.devices.reshape(tuple(dims.values())), tuple(dims))
    sizes = {**dims, "mp": dims["yl"] * dims["x"]}
    placed = (P(DP, None), P(DP), P(DP))
    return jax.shard_map(
        functools.partial(shards, sizes),
        mesh=finer,
        in_specs=placed,
        out_specs=(P(DP), P(DP, None)),
        check_vma=False,
    )
```

```python
import functools

import jax
import jax.numpy as jnp
from jax import lax
from jax.experimental import pallas as pl
from jax.experimental.pallas import tpu as pltpu
from jax.sharding import Mesh
from jax.sharding import PartitionSpec as P


INV_TAU = 10.0
EPS = 1e-06
LOG2E = 1.4426950408889634

DP = ("zh", "zl", "yh", "core")
MP = ("x", "yl")
FAR = ("yh", "zh")
TEAM = ("zl", "x", "yl")
OWNERS = ("core", "yh", "zh")

BLOCK = 256
NT = (((1,), (1,)), ((), ()))


def swap(x, axis):
    return lax.ppermute(x, axis, [(0, 1), (1, 0)])


def exchange(x, axes):
    return lax.all_to_all(x, axes, 0, 0, tiled=True)


def scaled(x):
    floats = x.astype(jnp.float32)
    length = jnp.sqrt(jnp.sum(floats * floats, axis=1, keepdims=True) + EPS)
    return floats, length, 1.0 / length


def place():
    zh, zl, yh, core = (lax.axis_index(a) for a in DP)
    return zh, zl, yh, core, lax.axis_index(MP)


def chunk_scalars(at, q, near, piece, sizes):
    zh, zl, yh, core, slot = at
    its_core = 1 - core if near else core
    its_yh, its_zh = q // sizes["zh"], q % sizes["zh"]
    group = ((its_zh * sizes["zl"] + zl) * sizes["yh"] + its_yh) * sizes["core"] + its_core
    base = (group * sizes["mp"] + slot) * piece
    if near:
        return base, None
    mine = jnp.logical_and(yh == its_yh, zh == its_zh)
    return base, jnp.where(mine, slot * piece, -(1 << 20))


def partner_ids(own_ref, oth_ref, rows):
    ids = []
    for ref in (own_ref, oth_ref):
        pair = ref[pl.ds(rows, 8), :].astype(jnp.float32)
        pair = (pair[0:2] * 256.0 + pair[2:4]).astype(jnp.int32)
        ids += [pair[n : n + 1] for n in range(pair.shape[0])]
    return jnp.concatenate(ids, axis=1)


def pack_kernel(views, part, weight, own, spread, heft, mates, arrived):
    rows = views.shape[0]
    piece = spread.shape[1]
    copy = pltpu.make_async_copy(views, own.at[pl.ds(0, rows)], arrived.at[0])
    small = pltpu.make_async_copy(part, mates, arrived.at[1])
    last = pltpu.make_async_copy(weight, heft, arrived.at[2])
    small.start()
    copy.start()
    last.start()
    small.wait()
    ids = mates[...]
    half_row = rows // 2
    parts = [x[:, n * half_row : (n + 1) * half_row] for x in (ids >> 8, ids & 255) for n in (0, 1)]
    blank = jnp.zeros((own.shape[0] - rows - 4, half_row), jnp.int32)
    packed = jnp.concatenate(parts + [blank], axis=0).astype(jnp.float32)
    own[pl.ds(rows, own.shape[0] - rows), :] = packed.astype(jnp.bfloat16)
    slot = lax.axis_index(MP)
    copy.wait()
    last.wait()
    mine = own[pl.ds(pl.multiple_of(slot * piece, piece), piece), :]
    for n in range(spread.shape[0]):
        spread[n] = mine


def forward_half(sizes, at, near, source, ids, nrow, ncol, e_out, s_buf, total, positive):
    chunks, piece = source.shape[0], source.shape[1]
    both = nrow.shape[0]
    rows = both // 2
    for q in range(chunks):
        floats, _, inverse = scaled(source[q])
        ncol[pl.ds(q * piece, piece), :] = (floats * inverse).astype(jnp.bfloat16)
    step = 8
    sub = lax.broadcasted_iota(jnp.int32, (step, both), 0)
    mates = jnp.broadcast_to(ids, (step, both)) - sub
    if not near:
        diag = lax.broadcasted_iota(jnp.int32, (step, rows), 1) - sub[:, :rows]
    right = nrow[...]
    for b in range(chunks * piece // BLOCK):
        s_buf[b % 2] = lax.dot_general(
            ncol[pl.ds(b * BLOCK, BLOCK), :], right, NT, preferred_element_type=jnp.float32
        )
        for c in range(BLOCK // piece):
            base, mine = chunk_scalars(at, b * (BLOCK // piece) + c, near, piece, sizes)
            for r in range(0, piece, step):
                s = s_buf[b % 2, pl.ds(c * piece + r, step), :]
                e = jnp.exp2(s * (INV_TAU * LOG2E))
                if mine is not None:
                    first = jnp.where(diag == mine + r, 0.0, e[:, :rows])
                    e = jnp.concatenate([first, e[:, rows:]], axis=1)
                e_out[pl.ds(b * BLOCK + c * piece + r, step), :] = e
                total = total + e
                positive = jnp.where(mates == base + r, s, positive)
    return total, positive


def far_kernel(sizes, own, oth, far, sums, ncol, nrow, e_out, s_buf):
    rows = nrow.shape[0] // 2
    for at, source in ((0, own[0:rows, :]), (rows, oth[0:rows, :])):
        floats, _, inverse = scaled(source)
        nrow[pl.ds(at, rows), :] = (floats * inverse).astype(jnp.bfloat16)
    ids = partner_ids(own, oth, rows)
    zero = jnp.zeros((8, 2 * rows), jnp.float32)
    total, positive = forward_half(
        sizes, place(), False, far, ids, nrow, ncol, e_out, s_buf, zero, zero
    )
    sums[0] = total
    sums[1] = positive


def near_kernel(sizes, own, oth, near, weight, sums, nrow, msg, ncol, e_out, s_buf):
    rows = nrow.shape[0] // 2
    at = place()
    ids = partner_ids(own, oth, rows)
    total, positive = forward_half(
        sizes, at, True, near, ids, nrow, ncol, e_out, s_buf, sums[0], sums[1]
    )
    total = jnp.sum(total, axis=0, keepdims=True)
    positive = jnp.sum(positive, axis=0, keepdims=True) * INV_TAU
    zl = at[1]
    same = [total[:, :rows], total[:, rows:], positive[:, :rows], weight[...]]
    turned = [total[:, rows:], total[:, :rows], positive[:, rows:], weight[...]]
    half_row = rows // 2

    def stacked(parts):
        return jnp.concatenate(
            [p[:, n * half_row : (n + 1) * half_row] for p in parts for n in range(2)], axis=0
        )

    same, turned = stacked(same), stacked(turned)
    members = sizes["mp"]
    for n in range(members):
        msg[zl * members + n] = same
        msg[(1 - zl) * members + n] = turned


def totals_kernel(sizes, got, weight, info, loss, cw):
    _, zl, _, _, slot = place()
    members = sizes["mp"]
    summed = got[0]
    for n in range(1, got.shape[0]):
        summed = summed + got[n]
    other_weight = got[(1 - zl) * members, 6:8, :]

    def joined(pair):
        return jnp.concatenate([pair[0:1], pair[1:2]], axis=1)

    total, total_other = joined(summed[0:2]), joined(summed[2:4])
    positive = joined(summed[4:6])
    other_weight = joined(other_weight)
    own_weight = weight[...]
    share = own_weight / total
    share_other = other_weight / total_other
    loss[...] = jnp.log(total) - positive
    info[...] = jnp.concatenate([share, share_other, own_weight, other_weight], axis=0)
    piece = own_weight.shape[1] // members
    out = jnp.zeros((1, 2 * piece), jnp.float32)
    for n in range(members):
        at = slice(n * piece, (n + 1) * piece)
        out = jnp.where(slot == n, jnp.concatenate([share[:, at], own_weight[:, at]], axis=1), out)
    for n in range(cw.shape[0]):
        cw[n] = out


def backward_kernel(
    sizes, own, oth, ncol_far, ncol_near, e_far, e_near, info, cw, msg, coef, acc
):
    both, width = acc.shape[1], acc.shape[0]
    rows = both // 2
    chunks = cw.shape[0] // 2
    half = ncol_far.shape[0]
    piece = half // chunks
    step = 16
    at = place()
    ids = partner_ids(own, oth, rows)
    mates = jnp.broadcast_to(ids, (step, both)) - lax.broadcasted_iota(jnp.int32, (step, both), 0)
    row_share = jnp.concatenate([info[0:1, :], info[1:2, :]], axis=1)
    row_weight = jnp.concatenate([info[2:3, :], info[3:4, :]], axis=1)
    row_share = jnp.broadcast_to(row_share, (step, both))
    row_weight = jnp.broadcast_to(row_weight, (step, both))
    turn = 0
    for near, ncol, e_ref in ((False, ncol_far, e_far), (True, ncol_near, e_near)):
        core = 1 - at[3] if near else at[3]
        columns = cw[pl.ds(core * chunks, chunks)].reshape(chunks, 2 * piece).T
        for b in range(half // BLOCK):
            for c in range(BLOCK // piece):
                q = b * (BLOCK // piece) + c
                base, _ = chunk_scalars(at, q, near, piece, sizes)
                column = columns[:, q : q + 1]
                for r in range(0, piece, step):
                    e = e_ref[pl.ds(b * BLOCK + c * piece + r, step), :]
                    value = e * (row_share + column[r : r + step])
                    pull = row_weight + column[piece + r : piece + r + step]
                    value = jnp.where(mates == base + r, value - pull, value)
                    coef[turn % 2, pl.ds(c * piece + r, step), :] = value.astype(jnp.bfloat16)
            left = ncol[pl.ds(b * BLOCK, BLOCK), :].T
            product = jnp.dot(left, coef[turn % 2], preferred_element_type=jnp.float32)
            if turn == 0:
                acc[...] = product
            else:
                acc[...] += product
            turn += 1
    zl = at[1]
    members = sizes["mp"]
    for to, first, source in ((zl, 0, own[0:rows, :]), (1 - zl, rows, oth[0:rows, :])):
        floats, _, inverse = scaled(source)
        g = acc[:, first : first + rows].T * INV_TAU
        unit = floats * inverse
        out = (g - unit * jnp.sum(unit * g, axis=1, keepdims=True)) * inverse
        msg[pl.ds(to * members, members)] = out.astype(jnp.bfloat16).reshape(members, -1, width)


def finish_kernel(got, out, wide, stored):
    piece = got.shape[1]
    copies = []
    for n in range(got.shape[0]):
        at = pl.ds(n * piece, piece)
        wide[at, :] = got[n].astype(jnp.float32)
        copies.append(pltpu.make_async_copy(wide.at[at], out.at[at], stored.at[n]))
        copies[-1].start()
    for copy in copies:
        copy.wait()


def call(kernel, outs, args, scratch=(), mib=4, flops=0):
    vmem = pl.BlockSpec(memory_space=pltpu.VMEM)
    return pl.pallas_call(
        kernel,
        in_specs=[vmem] * len(args),
        out_specs=[vmem] * len(outs),
        out_shape=[jax.ShapeDtypeStruct(*o) for o in outs],
        scratch_shapes=list(scratch),
        compiler_params=pltpu.CompilerParams(vmem_limit_bytes=mib << 20),
        cost_estimate=pl.CostEstimate(flops=flops, bytes_accessed=1 << 20, transcendentals=0),
    )(*args)


def shards(sizes, views, partner, weight):
    return body(sizes, views, partner, weight)


def body(sizes, views, partner, weight):
    rows, width = views.shape
    members = sizes["mp"]
    piece = rows // members
    f32, bf16 = jnp.float32, jnp.bfloat16

    chunks = sizes["zh"] * sizes["yh"]
    own, spread, heft = pl.pallas_call(
        pack_kernel,
        name="pack",
        in_specs=[pl.BlockSpec(memory_space=pltpu.HBM)] * 3,
        out_specs=[pl.BlockSpec(memory_space=pltpu.VMEM)] * 3,
        out_shape=[
            jax.ShapeDtypeStruct((rows + 16, width), bf16),
            jax.ShapeDtypeStruct((chunks, piece, width), bf16),
            jax.ShapeDtypeStruct((1, rows), f32),
        ],
        scratch_shapes=[pltpu.VMEM((1, rows), jnp.int32), pltpu.SemaphoreType.DMA((3,))],
        compiler_params=pltpu.CompilerParams(vmem_limit_bytes=4 << 20),
    )(*[
        pltpu.with_memory_space_constraint(a, pltpu.HBM)
        for a in (views, partner.reshape(1, rows), weight.reshape(1, rows))
    ])
    oth = swap(own, "zl")
    far = exchange(spread, FAR)
    near = swap(far, "core")

    half, both, team = chunks * piece, 2 * rows, 2 * members
    flops = 2 * half * both * width
    score = pltpu.VMEM((2, BLOCK, both), f32)
    sums, ncol_far, nrow, e_far = call(
        functools.partial(far_kernel, sizes),
        [((2, 8, both), f32), ((half, width), bf16), ((both, width), bf16), ((half, both), f32)],
        (own, oth, far),
        [score],
        16,
        flops,
    )
    msg, ncol_near, e_near = call(
        functools.partial(near_kernel, sizes),
        [((team, 8, rows // 2), f32), ((half, width), bf16), ((half, both), f32)],
        (own, oth, near, heft, sums, nrow),
        [score],
        16,
        flops,
    )
    got = exchange(msg, TEAM)
    info, loss, cw = call(
        functools.partial(totals_kernel, sizes),
        [((4, rows), f32), ((1, rows), f32), ((2 * chunks, 1, 2 * piece), f32)],
        (got, heft),
    )
    cw = exchange(cw, OWNERS)
    (grads,) = call(
        functools.partial(backward_kernel, sizes),
        [((team, piece, width), bf16)],
        (own, oth, ncol_far, ncol_near, e_far, e_near, info, cw),
        [pltpu.VMEM((2, BLOCK, both), bf16), pltpu.VMEM((width, both), f32)],
        16,
        2 * flops,
    )
    shares = exchange(grads, TEAM)
    share = jnp.sum(shares.astype(f32), axis=0).astype(bf16)
    got = exchange(jnp.broadcast_to(share[None], (members, piece, width)), MP)
    grad = pl.pallas_call(
        finish_kernel,
        name="finish",
        in_specs=[pl.BlockSpec(memory_space=pltpu.VMEM)],
        out_specs=pl.BlockSpec(memory_space=pltpu.HBM),
        out_shape=jax.ShapeDtypeStruct((rows, width), f32),
        scratch_shapes=[pltpu.VMEM((rows, width), f32), pltpu.SemaphoreType.DMA((members,))],
        compiler_params=pltpu.CompilerParams(vmem_limit_bytes=4 << 20),
    )(got)
    return loss.reshape(rows), grad


def solution(mesh):
    dims = {"zh": 4, "zl": 2, "yh": 4, "core": 2, "yl": 2, "x": 4}
    finer = Mesh(mesh.devices.reshape(tuple(dims.values())), tuple(dims))
    sizes = {**dims, "mp": dims["yl"] * dims["x"]}
    placed = (P(DP, None), P(DP), P(DP))
    return jax.shard_map(
        functools.partial(shards, sizes),
        mesh=finer,
        in_specs=placed,
        out_specs=(P(DP), P(DP, None)),
        check_vma=False,
    )
```

```python
import functools

import jax
import jax.numpy as jnp
from jax import lax
from jax.experimental import pallas as pl
from jax.experimental.pallas import tpu as pltpu
from jax.sharding import Mesh
from jax.sharding import PartitionSpec as P


INV_TAU = 10.0
EPS = 1e-06
LOG2E = 1.4426950408889634

DP = ("zh", "zl", "yh", "core")
MP = ("x", "yl")
FAR = ("yh", "zh")
TEAM = ("zl", "x", "yl")
OWNERS = ("core", "yh", "zh")

BLOCK = 256
NT = (((1,), (1,)), ((), ()))


def swap(x, axis):
    return lax.ppermute(x, axis, [(0, 1), (1, 0)])


def exchange(x, axes):
    return lax.all_to_all(x, axes, 0, 0, tiled=True)


def scaled(x):
    floats = x.astype(jnp.float32)
    length = jnp.sqrt(jnp.sum(floats * floats, axis=1, keepdims=True) + EPS)
    return floats, length, 1.0 / length


def place():
    zh, zl, yh, core = (lax.axis_index(a) for a in DP)
    return zh, zl, yh, core, lax.axis_index(MP)


def chunk_scalars(at, q, near, piece, sizes):
    zh, zl, yh, core, slot = at
    its_core = 1 - core if near else core
    its_yh, its_zh = q // sizes["zh"], q % sizes["zh"]
    group = ((its_zh * sizes["zl"] + zl) * sizes["yh"] + its_yh) * sizes["core"] + its_core
    base = (group * sizes["mp"] + slot) * piece
    if near:
        return base, None
    mine = jnp.logical_and(yh == its_yh, zh == its_zh)
    return base, jnp.where(mine, slot * piece, -(1 << 20))


def triple(x):
    high = x.astype(jnp.bfloat16).astype(jnp.float32)
    rest = x - high
    middle = rest.astype(jnp.bfloat16).astype(jnp.float32)
    return high, middle, rest - middle


def row_weights(refs, rows):
    parts = []
    for ref in refs:
        tail = ref[pl.ds(rows, 16), :].astype(jnp.float32)
        pair = tail[4:6] + tail[6:8] + tail[8:10]
        parts += [pair[n : n + 1] for n in range(pair.shape[0])]
    return jnp.concatenate(parts, axis=1)


def chosen(row, slot, piece):
    mine = row[:, :piece]
    for n in range(1, row.shape[1] // piece):
        mine = jnp.where(slot == n, row[:, n * piece : (n + 1) * piece], mine)
    return mine


def partner_ids(own_ref, oth_ref, rows):
    ids = []
    for ref in (own_ref, oth_ref):
        pair = ref[pl.ds(rows, 8), :].astype(jnp.float32)
        pair = (pair[0:2] * 256.0 + pair[2:4]).astype(jnp.int32)
        ids += [pair[n : n + 1] for n in range(pair.shape[0])]
    return jnp.concatenate(ids, axis=1)


def pack_kernel(views, part, weight, own, spread, heft, mates, arrived):
    rows = views.shape[0]
    piece = spread.shape[1]
    copy = pltpu.make_async_copy(views, own.at[pl.ds(0, rows)], arrived.at[0])
    small = pltpu.make_async_copy(part, mates, arrived.at[1])
    last = pltpu.make_async_copy(weight, heft, arrived.at[2])
    small.start()
    copy.start()
    last.start()
    small.wait()
    ids = mates[...]
    half_row = rows // 2
    parts = [x[:, n * half_row : (n + 1) * half_row] for x in (ids >> 8, ids & 255) for n in (0, 1)]
    parts = [x.astype(jnp.float32) for x in parts]
    last.wait()
    for x in triple(heft[...]):
        parts += [x[:, n * half_row : (n + 1) * half_row] for n in (0, 1)]
    parts.append(jnp.zeros((own.shape[0] - rows - len(parts), half_row), jnp.float32))
    packed = jnp.concatenate(parts, axis=0)
    own[pl.ds(rows, own.shape[0] - rows), :] = packed.astype(jnp.bfloat16)
    slot = lax.axis_index(MP)
    copy.wait()
    mine = own[pl.ds(pl.multiple_of(slot * piece, piece), piece), :]
    for n in range(spread.shape[0]):
        spread[n] = mine


def forward_half(
    sizes, at, near, source, ids, nrow, ncol, e_out, s_buf, lanes, total, positive
):
    chunks, piece = source.shape[0], source.shape[1]
    both = nrow.shape[0]
    rows = both // 2
    for q in range(chunks):
        floats, _, inverse = scaled(source[q])
        ncol[pl.ds(q * piece, piece), :] = (floats * inverse).astype(jnp.bfloat16)
    step = 8
    sub = lax.broadcasted_iota(jnp.int32, (step, both), 0)
    mates = jnp.broadcast_to(ids, (step, both)) - sub
    if not near:
        diag = lax.broadcasted_iota(jnp.int32, (step, rows), 1) - sub[:, :rows]
    right = nrow[...]
    for b in range(chunks * piece // BLOCK):
        s_buf[b % 2] = lax.dot_general(
            ncol[pl.ds(b * BLOCK, BLOCK), :], right, NT, preferred_element_type=jnp.float32
        )
        for c in range(BLOCK // piece):
            base, mine = chunk_scalars(at, b * (BLOCK // piece) + c, near, piece, sizes)
            for r in range(0, piece, step):
                s = s_buf[b % 2, pl.ds(c * piece + r, step), :]
                e = jnp.exp2(s * (INV_TAU * LOG2E))
                if mine is not None:
                    first = jnp.where(diag == mine + r, 0.0, e[:, :rows])
                    e = jnp.concatenate([first, e[:, rows:]], axis=1)
                here = pl.ds(b * BLOCK + c * piece + r, step)
                e_out[here, :] = e
                across = e[:, :128]
                for n in range(128, both, 128):
                    across = across + e[:, n : n + 128]
                lanes[here, :] = across
                total = total + e
                positive = jnp.where(mates == base + r, s, positive)
    column = [
        jnp.sum(lanes[n : n + 128, :].T, axis=0, keepdims=True)
        for n in range(0, chunks * piece, 128)
    ]
    return total, positive, jnp.concatenate(column, axis=0)


def far_kernel(sizes, own, oth, far, sums, column, ncol, nrow, e_out, s_buf, lanes):
    rows = nrow.shape[0] // 2
    for at, source in ((0, own[0:rows, :]), (rows, oth[0:rows, :])):
        floats, _, inverse = scaled(source)
        nrow[pl.ds(at, rows), :] = (floats * inverse).astype(jnp.bfloat16)
    ids = partner_ids(own, oth, rows)
    zero = jnp.zeros((8, 2 * rows), jnp.float32)
    total, positive, column[...] = forward_half(
        sizes, place(), False, far, ids, nrow, ncol, e_out, s_buf, lanes, zero, zero
    )
    sums[0] = total
    sums[1] = positive


def near_kernel(
    sizes, own, oth, near, weight, sums, column, nrow, scores, cmsg, ncol, e_out, s_buf, lanes
):
    rows = nrow.shape[0] // 2
    at = place()
    ids = partner_ids(own, oth, rows)
    total, positive, last = forward_half(
        sizes, at, True, near, ids, nrow, ncol, e_out, s_buf, lanes, sums[0], sums[1]
    )
    total = jnp.sum(total, axis=0, keepdims=True)
    positive = jnp.sum(positive, axis=0, keepdims=True) * INV_TAU
    scores[...] = jnp.concatenate([total, positive], axis=0)
    piece = rows // sizes["mp"]
    core, slot = at[3], at[4]
    mine = chosen(weight[...], slot, piece)
    coarse = mine.astype(jnp.bfloat16).astype(jnp.float32)
    fine = jnp.concatenate([coarse, mine - coarse], axis=1)
    first = jnp.where(core == 0, column[...], last)
    second = jnp.where(core == 0, last, column[...])
    blank = jnp.zeros((7, 2 * piece), jnp.float32)
    packed = jnp.concatenate([first, second, fine, blank], axis=0).astype(jnp.bfloat16)
    for n in range(cmsg.shape[0]):
        cmsg[n] = packed


def backward_kernel(
    sizes, own, oth, ncol_far, ncol_near, e_far, e_near, scores, cgot, msg, near_coef, coef, acc
):
    both, width = acc.shape[2], acc.shape[1]
    rows = both // 2
    chunks = cgot.shape[0] // 2
    half = ncol_far.shape[0]
    piece = half // chunks
    step = 16
    at = place()
    ids = partner_ids(own, oth, rows)
    mates = jnp.broadcast_to(ids, (step, both)) - lax.broadcasted_iota(jnp.int32, (step, both), 0)
    row_weight = jnp.broadcast_to(row_weights((own, oth), rows), (step, both))
    column_total = cgot[0, 0:16, :].astype(jnp.float32)
    for n in range(1, 2 * chunks):
        column_total = column_total + cgot[n, 0:16, :].astype(jnp.float32)
    inverse_total = 1.0 / column_total
    turn = 0
    for near, ncol, e_ref in ((False, ncol_far, e_far), (True, ncol_near, e_near)):
        core = 1 - at[3] if near else at[3]
        inverse = jnp.where(core == 0, inverse_total[0:8], inverse_total[8:16]).T
        heft = []
        for q in range(chunks):
            row = cgot[core * chunks + q, 16:24, :].astype(jnp.float32)[0:1]
            heft.append(row + jnp.concatenate([row[:, piece:], row[:, :piece]], axis=1))
        heft = jnp.concatenate(heft, axis=0).T
        for b in range(half // BLOCK):
            for c in range(BLOCK // piece):
                q = b * (BLOCK // piece) + c
                base, _ = chunk_scalars(at, q, near, piece, sizes)
                odd = slice(q % 2 * piece, (q % 2 + 1) * piece)
                pull_in = heft[odd, q : q + 1]
                column = pull_in * inverse[odd, q // 2 : q // 2 + 1]
                for r in range(0, piece, step):
                    here = pl.ds(c * piece + r, step)
                    e = e_ref[pl.ds(b * BLOCK + c * piece + r, step), :]
                    near_coef[turn % 2, here, :] = e.astype(jnp.bfloat16)
                    value = e * column[r : r + step]
                    pull = row_weight + pull_in[r : r + step]
                    value = jnp.where(mates == base + r, value - pull, value)
                    coef[turn % 2, here, :] = value.astype(jnp.bfloat16)
            left = ncol[pl.ds(b * BLOCK, BLOCK), :].T
            for which, right in enumerate((near_coef, coef)):
                product = jnp.dot(left, right[turn % 2], preferred_element_type=jnp.float32)
                if turn == 0:
                    acc[which] = product
                else:
                    acc[which] += product
            turn += 1
    zl = at[1]
    members = sizes["mp"]
    own_rows = rows // members
    none = jnp.zeros((1, width - 3 * own_rows), jnp.float32)
    blank = jnp.zeros((6, width), jnp.float32)
    for to, first, source in ((zl, 0, own[0:rows, :]), (1 - zl, rows, oth[0:rows, :])):
        floats, _, inverse = scaled(source)
        unit = floats * inverse
        lot = pl.ds(to * members, members)
        for which in range(2):
            g = acc[which, :, first : first + rows].T * INV_TAU
            out = (g - unit * jnp.sum(unit * g, axis=1, keepdims=True)) * inverse
            out = out.astype(jnp.bfloat16).reshape(members, own_rows, width)
            msg[lot, which * own_rows : (which + 1) * own_rows, :] = out
        pieces = [triple(scores[n : n + 1, first : first + rows]) for n in range(2)]
        for n in range(members):
            cut = slice(n * own_rows, (n + 1) * own_rows)
            lines = [jnp.concatenate([p[:, cut] for p in x] + [none], axis=1) for x in pieces]
            extra = jnp.concatenate(lines + [blank], axis=0).astype(jnp.bfloat16)
            msg[to * members + n, 2 * own_rows : 2 * own_rows + 8, :] = extra


def owner_kernel(sizes, own, got, out):
    piece = (got.shape[1] - 8) // 2
    width = got.shape[2]
    rows = piece * sizes["mp"]
    slot = place()[4]
    first, second, extra = (
        got[0, lo:hi, :].astype(jnp.float32)
        for lo, hi in ((0, piece), (piece, 2 * piece), (2 * piece, 2 * piece + 8))
    )
    for n in range(1, got.shape[0]):
        first = first + got[n, 0:piece, :].astype(jnp.float32)
        second = second + got[n, piece : 2 * piece, :].astype(jnp.float32)
        extra = extra + got[n, 2 * piece : 2 * piece + 8, :].astype(jnp.float32)
    extra = extra[:, :piece] + extra[:, piece : 2 * piece] + extra[:, 2 * piece : 3 * piece]
    total, positive = extra[0:1], extra[1:2]
    share = chosen(row_weights((own,), rows), slot, piece) / total
    share = jnp.concatenate([share, share], axis=1)
    share = jnp.broadcast_to(share, (8, 2 * piece)).T[0:piece, 0:1]
    grad = (first * share + second).astype(jnp.bfloat16)
    loss = jnp.log(total) - positive
    none = jnp.zeros((1, width - 3 * piece), jnp.float32)
    line = jnp.concatenate([*triple(loss), none], axis=1)
    line = jnp.concatenate([line, jnp.zeros((7, width), jnp.float32)], axis=0)
    line = line.astype(jnp.bfloat16)
    for n in range(out.shape[0]):
        out[n, 0:piece, :] = grad
        out[n, piece : piece + 8, :] = line


def finish_kernel(got, out, loss, wide, stored):
    piece = got.shape[1] - 8
    copies, losses = [], []
    for n in range(got.shape[0]):
        at = pl.ds(n * piece, piece)
        wide[at, :] = got[n, 0:piece, :].astype(jnp.float32)
        copies.append(pltpu.make_async_copy(wide.at[at], out.at[at], stored.at[n]))
        copies[-1].start()
        line = got[n, piece : piece + 8, :].astype(jnp.float32)[0:1]
        losses.append(line[:, :piece] + line[:, piece : 2 * piece] + line[:, 2 * piece : 3 * piece])
    loss[...] = jnp.concatenate(losses, axis=1)
    for copy in copies:
        copy.wait()


def call(kernel, outs, args, scratch=(), mib=4, flops=0):
    vmem = pl.BlockSpec(memory_space=pltpu.VMEM)
    return pl.pallas_call(
        kernel,
        in_specs=[vmem] * len(args),
        out_specs=[vmem] * len(outs),
        out_shape=[jax.ShapeDtypeStruct(*o) for o in outs],
        scratch_shapes=list(scratch),
        compiler_params=pltpu.CompilerParams(vmem_limit_bytes=mib << 20),
        cost_estimate=pl.CostEstimate(flops=flops, bytes_accessed=1 << 20, transcendentals=0),
    )(*args)


def shards(sizes, views, partner, weight):
    return body(sizes, views, partner, weight)


def body(sizes, views, partner, weight):
    rows, width = views.shape
    members = sizes["mp"]
    piece = rows // members
    f32, bf16 = jnp.float32, jnp.bfloat16

    chunks = sizes["zh"] * sizes["yh"]
    own, spread, heft = pl.pallas_call(
        pack_kernel,
        name="pack",
        in_specs=[pl.BlockSpec(memory_space=pltpu.HBM)] * 3,
        out_specs=[pl.BlockSpec(memory_space=pltpu.VMEM)] * 3,
        out_shape=[
            jax.ShapeDtypeStruct((rows + 16, width), bf16),
            jax.ShapeDtypeStruct((chunks, piece, width), bf16),
            jax.ShapeDtypeStruct((1, rows), f32),
        ],
        scratch_shapes=[pltpu.VMEM((1, rows), jnp.int32), pltpu.SemaphoreType.DMA((3,))],
        compiler_params=pltpu.CompilerParams(vmem_limit_bytes=4 << 20),
    )(*[
        pltpu.with_memory_space_constraint(a, pltpu.HBM)
        for a in (views, partner.reshape(1, rows), weight.reshape(1, rows))
    ])
    oth = swap(own, "zl")
    far = exchange(spread, FAR)
    near = swap(far, "core")

    half, both, team = chunks * piece, 2 * rows, 2 * members
    flops = 2 * half * both * width
    scratch = [pltpu.VMEM((2, BLOCK, both), f32), pltpu.VMEM((half, 128), f32)]
    sums, column, ncol_far, nrow, e_far = call(
        functools.partial(far_kernel, sizes),
        [
            ((2, 8, both), f32),
            ((half // 128, 128), f32),
            ((half, width), bf16),
            ((both, width), bf16),
            ((half, both), f32),
        ],
        (own, oth, far),
        scratch,
        16,
        flops,
    )
    scores, cmsg, ncol_near, e_near = call(
        functools.partial(near_kernel, sizes),
        [
            ((2, both), f32),
            ((2 * chunks, 24, 128), bf16),
            ((half, width), bf16),
            ((half, both), f32),
        ],
        (own, oth, near, heft, sums, column, nrow),
        scratch,
        16,
        flops,
    )
    cgot = exchange(cmsg, OWNERS)
    (msg,) = call(
        functools.partial(backward_kernel, sizes),
        [((team, 2 * piece + 8, width), bf16)],
        (own, oth, ncol_far, ncol_near, e_far, e_near, scores, cgot),
        [pltpu.VMEM((2, BLOCK, both), bf16)] * 2 + [pltpu.VMEM((2, width, both), f32)],
        16,
        4 * flops,
    )
    got = exchange(msg, TEAM)
    (share,) = call(
        functools.partial(owner_kernel, sizes), [((members, piece + 8, width), bf16)], (own, got)
    )
    got = exchange(share, MP)
    grad, loss = pl.pallas_call(
        finish_kernel,
        name="finish",
        in_specs=[pl.BlockSpec(memory_space=pltpu.VMEM)],
        out_specs=[pl.BlockSpec(memory_space=pltpu.HBM), pl.BlockSpec(memory_space=pltpu.VMEM)],
        out_shape=[
            jax.ShapeDtypeStruct((rows, width), f32),
            jax.ShapeDtypeStruct((1, rows), f32),
        ],
        scratch_shapes=[pltpu.VMEM((rows, width), f32), pltpu.SemaphoreType.DMA((members,))],
        compiler_params=pltpu.CompilerParams(vmem_limit_bytes=4 << 20),
    )(got)
    return loss.reshape(rows), grad


def solution(mesh):
    dims = {"zh": 4, "zl": 2, "yh": 4, "core": 2, "yl": 2, "x": 4}
    finer = Mesh(mesh.devices.reshape(tuple(dims.values())), tuple(dims))
    sizes = {**dims, "mp": dims["yl"] * dims["x"]}
    placed = (P(DP, None), P(DP), P(DP))
    return jax.shard_map(
        functools.partial(shards, sizes),
        mesh=finer,
        in_specs=placed,
        out_specs=(P(DP), P(DP, None)),
        check_vma=False,
    )
```

```python
import functools

import jax
import jax.numpy as jnp
from jax import lax
from jax.experimental import pallas as pl
from jax.experimental.pallas import tpu as pltpu
from jax.sharding import Mesh
from jax.sharding import PartitionSpec as P


INV_TAU = 10.0
EPS = 1e-06
LOG2E = 1.4426950408889634

DP = ("zh", "zl", "yh", "core")
MP = ("x", "yl")
FAR = ("yh", "zh")
TEAM = ("zl", "x", "yl")
OWNERS = ("core", "yh", "zh")

BLOCK = 256
NT = (((1,), (1,)), ((), ()))


def swap(x, axis):
    return lax.ppermute(x, axis, [(0, 1), (1, 0)])


def exchange(x, axes):
    return lax.all_to_all(x, axes, 0, 0, tiled=True)


def scaled(x):
    floats = x.astype(jnp.float32)
    length = jnp.sqrt(jnp.sum(floats * floats, axis=1, keepdims=True) + EPS)
    return floats, length, 1.0 / length


def place():
    zh, zl, yh, core = (lax.axis_index(a) for a in DP)
    return zh, zl, yh, core, lax.axis_index(MP)


def chunk_scalars(at, q, near, piece, sizes):
    zh, zl, yh, core, slot = at
    its_core = 1 - core if near else core
    its_yh, its_zh = q // sizes["zh"], q % sizes["zh"]
    group = ((its_zh * sizes["zl"] + zl) * sizes["yh"] + its_yh) * sizes["core"] + its_core
    base = (group * sizes["mp"] + slot) * piece
    if near:
        return base, None
    mine = jnp.logical_and(yh == its_yh, zh == its_zh)
    return base, jnp.where(mine, slot * piece, -(1 << 20))


def partner_ids(own_ref, oth_ref, rows):
    ids = []
    for ref in (own_ref, oth_ref):
        pair = ref[pl.ds(rows, 8), :].astype(jnp.float32)
        pair = (pair[0:2] * 256.0 + pair[2:4]).astype(jnp.int32)
        ids += [pair[n : n + 1] for n in range(pair.shape[0])]
    return jnp.concatenate(ids, axis=1)


def pack_kernel(views, part, weight, own, spread, heft, mates, arrived):
    rows = views.shape[0]
    piece = spread.shape[1]
    copy = pltpu.make_async_copy(views, own.at[pl.ds(0, rows)], arrived.at[0])
    small = pltpu.make_async_copy(part, mates, arrived.at[1])
    last = pltpu.make_async_copy(weight, heft, arrived.at[2])
    small.start()
    copy.start()
    last.start()
    small.wait()
    ids = mates[...]
    half_row = rows // 2
    parts = [x[:, n * half_row : (n + 1) * half_row] for x in (ids >> 8, ids & 255) for n in (0, 1)]
    blank = jnp.zeros((own.shape[0] - rows - 4, half_row), jnp.int32)
    packed = jnp.concatenate(parts + [blank], axis=0).astype(jnp.float32)
    own[pl.ds(rows, own.shape[0] - rows), :] = packed.astype(jnp.bfloat16)
    slot = lax.axis_index(MP)
    copy.wait()
    last.wait()
    mine = own[pl.ds(pl.multiple_of(slot * piece, piece), piece), :]
    for n in range(spread.shape[0]):
        spread[n] = mine


def forward_half(sizes, at, near, source, ids, nrow, ncol, e_out, s_buf, total, positive):
    chunks, piece = source.shape[0], source.shape[1]
    both = nrow.shape[0]
    rows = both // 2
    for q in range(chunks):
        floats, _, inverse = scaled(source[q])
        ncol[pl.ds(q * piece, piece), :] = (floats * inverse).astype(jnp.bfloat16)
    step = 8
    sub = lax.broadcasted_iota(jnp.int32, (step, both), 0)
    mates = jnp.broadcast_to(ids, (step, both)) - sub
    if not near:
        diag = lax.broadcasted_iota(jnp.int32, (step, rows), 1) - sub[:, :rows]
    right = nrow[...]
    for b in range(chunks * piece // BLOCK):
        s_buf[b % 2] = lax.dot_general(
            ncol[pl.ds(b * BLOCK, BLOCK), :], right, NT, preferred_element_type=jnp.float32
        )
        for c in range(BLOCK // piece):
            base, mine = chunk_scalars(at, b * (BLOCK // piece) + c, near, piece, sizes)
            for r in range(0, piece, step):
                s = s_buf[b % 2, pl.ds(c * piece + r, step), :]
                e = jnp.exp2(s * (INV_TAU * LOG2E))
                if mine is not None:
                    first = jnp.where(diag == mine + r, 0.0, e[:, :rows])
                    e = jnp.concatenate([first, e[:, rows:]], axis=1)
                e_out[pl.ds(b * BLOCK + c * piece + r, step), :] = e
                total = total + e
                positive = jnp.where(mates == base + r, s, positive)
    return total, positive


def far_kernel(sizes, own, oth, far, sums, ncol, nrow, e_out, s_buf):
    rows = nrow.shape[0] // 2
    for at, source in ((0, own[0:rows, :]), (rows, oth[0:rows, :])):
        floats, _, inverse = scaled(source)
        nrow[pl.ds(at, rows), :] = (floats * inverse).astype(jnp.bfloat16)
    ids = partner_ids(own, oth, rows)
    zero = jnp.zeros((8, 2 * rows), jnp.float32)
    total, positive = forward_half(
        sizes, place(), False, far, ids, nrow, ncol, e_out, s_buf, zero, zero
    )
    sums[0] = total
    sums[1] = positive


def near_kernel(sizes, own, oth, near, weight, sums, nrow, msg, ncol, e_out, s_buf):
    rows = nrow.shape[0] // 2
    at = place()
    ids = partner_ids(own, oth, rows)
    total, positive = forward_half(
        sizes, at, True, near, ids, nrow, ncol, e_out, s_buf, sums[0], sums[1]
    )
    total = jnp.sum(total, axis=0, keepdims=True)
    positive = jnp.sum(positive, axis=0, keepdims=True) * INV_TAU
    zl = at[1]
    same = [total[:, :rows], total[:, rows:], positive[:, :rows], weight[...]]
    turned = [total[:, rows:], total[:, :rows], positive[:, rows:], weight[...]]
    half_row = rows // 2

    def stacked(parts):
        return jnp.concatenate(
            [p[:, n * half_row : (n + 1) * half_row] for p in parts for n in range(2)], axis=0
        )

    same, turned = stacked(same), stacked(turned)
    members = sizes["mp"]
    for n in range(members):
        msg[zl * members + n] = same
        msg[(1 - zl) * members + n] = turned


def totals_kernel(sizes, got, weight, info, loss, cw):
    _, zl, _, _, slot = place()
    members = sizes["mp"]
    summed = got[0]
    for n in range(1, got.shape[0]):
        summed = summed + got[n]
    other_weight = got[(1 - zl) * members, 6:8, :]

    def joined(pair):
        return jnp.concatenate([pair[0:1], pair[1:2]], axis=1)

    total, total_other = joined(summed[0:2]), joined(summed[2:4])
    positive = joined(summed[4:6])
    other_weight = joined(other_weight)
    own_weight = weight[...]
    share = own_weight / total
    share_other = other_weight / total_other
    loss[...] = jnp.log(total) - positive
    info[...] = jnp.concatenate([share, share_other, own_weight, other_weight], axis=0)
    piece = own_weight.shape[1] // members
    out = jnp.zeros((1, 2 * piece), jnp.float32)
    for n in range(members):
        at = slice(n * piece, (n + 1) * piece)
        out = jnp.where(slot == n, jnp.concatenate([share[:, at], own_weight[:, at]], axis=1), out)
    for n in range(cw.shape[0]):
        cw[n] = out


def backward_kernel(
    sizes, own, oth, ncol_far, ncol_near, e_far, e_near, info, cw, msg, coef, acc
):
    both, width = acc.shape[1], acc.shape[0]
    rows = both // 2
    chunks = cw.shape[0] // 2
    half = ncol_far.shape[0]
    piece = half // chunks
    step = 16
    at = place()
    ids = partner_ids(own, oth, rows)
    mates = jnp.broadcast_to(ids, (step, both)) - lax.broadcasted_iota(jnp.int32, (step, both), 0)
    row_share = jnp.concatenate([info[0:1, :], info[1:2, :]], axis=1)
    row_weight = jnp.concatenate([info[2:3, :], info[3:4, :]], axis=1)
    row_share = jnp.broadcast_to(row_share, (step, both))
    row_weight = jnp.broadcast_to(row_weight, (step, both))
    turn = 0
    for near, ncol, e_ref in ((False, ncol_far, e_far), (True, ncol_near, e_near)):
        core = 1 - at[3] if near else at[3]
        columns = cw[pl.ds(core * chunks, chunks)].reshape(chunks, 2 * piece).T
        for b in range(half // BLOCK):
            for c in range(BLOCK // piece):
                q = b * (BLOCK // piece) + c
                base, _ = chunk_scalars(at, q, near, piece, sizes)
                column = columns[:, q : q + 1]
                for r in range(0, piece, step):
                    e = e_ref[pl.ds(b * BLOCK + c * piece + r, step), :]
                    value = e * (row_share + column[r : r + step])
                    pull = row_weight + column[piece + r : piece + r + step]
                    value = jnp.where(mates == base + r, value - pull, value)
                    coef[turn, pl.ds(b * BLOCK + c * piece + r, step), :] = value.astype(jnp.bfloat16)
        product = jnp.dot(ncol[...].T, coef[turn], preferred_element_type=jnp.float32)
        if turn == 0:
            acc[...] = product
        else:
            acc[...] += product
        turn += 1
    zl = at[1]
    members = sizes["mp"]
    for to, first, source in ((zl, 0, own[0:rows, :]), (1 - zl, rows, oth[0:rows, :])):
        floats, _, inverse = scaled(source)
        g = acc[:, first : first + rows].T * INV_TAU
        unit = floats * inverse
        out = (g - unit * jnp.sum(unit * g, axis=1, keepdims=True)) * inverse
        msg[pl.ds(to * members, members)] = out.astype(jnp.bfloat16).reshape(members, -1, width)


def finish_kernel(got, loss, out, loss_out, wide, stored):
    piece = got.shape[1]
    copies = [pltpu.make_async_copy(loss, loss_out, stored.at[got.shape[0]])]
    copies[0].start()
    for n in range(got.shape[0]):
        at = pl.ds(n * piece, piece)
        wide[at, :] = got[n].astype(jnp.float32)
        copies.append(pltpu.make_async_copy(wide.at[at], out.at[at], stored.at[n]))
        copies[-1].start()
    for copy in copies:
        copy.wait()


def call(kernel, outs, args, scratch=(), mib=4, flops=0):
    vmem = pl.BlockSpec(memory_space=pltpu.VMEM)
    return pl.pallas_call(
        kernel,
        in_specs=[vmem] * len(args),
        out_specs=[vmem] * len(outs),
        out_shape=[jax.ShapeDtypeStruct(*o) for o in outs],
        scratch_shapes=list(scratch),
        compiler_params=pltpu.CompilerParams(vmem_limit_bytes=mib << 20),
        cost_estimate=pl.CostEstimate(flops=flops, bytes_accessed=1 << 20, transcendentals=0),
    )(*args)


def shards(sizes, views, partner, weight):
    return body(sizes, views, partner, weight)


def body(sizes, views, partner, weight):
    rows, width = views.shape
    members = sizes["mp"]
    piece = rows // members
    f32, bf16 = jnp.float32, jnp.bfloat16

    chunks = sizes["zh"] * sizes["yh"]
    own, spread, heft = pl.pallas_call(
        pack_kernel,
        name="pack",
        in_specs=[pl.BlockSpec(memory_space=pltpu.HBM)] * 3,
        out_specs=[pl.BlockSpec(memory_space=pltpu.VMEM)] * 3,
        out_shape=[
            jax.ShapeDtypeStruct((rows + 16, width), bf16),
            jax.ShapeDtypeStruct((chunks, piece, width), bf16),
            jax.ShapeDtypeStruct((1, rows), f32),
        ],
        scratch_shapes=[pltpu.VMEM((1, rows), jnp.int32), pltpu.SemaphoreType.DMA((3,))],
        compiler_params=pltpu.CompilerParams(vmem_limit_bytes=4 << 20),
    )(*[
        pltpu.with_memory_space_constraint(a, pltpu.HBM)
        for a in (views, partner.reshape(1, rows), weight.reshape(1, rows))
    ])
    oth = swap(own, "zl")
    far = exchange(spread, FAR)
    near = swap(far, "core")

    half, both, team = chunks * piece, 2 * rows, 2 * members
    flops = 2 * half * both * width
    score = pltpu.VMEM((2, BLOCK, both), f32)
    sums, ncol_far, nrow, e_far = call(
        functools.partial(far_kernel, sizes),
        [((2, 8, both), f32), ((half, width), bf16), ((both, width), bf16), ((half, both), f32)],
        (own, oth, far),
        [score],
        16,
        flops,
    )
    msg, ncol_near, e_near = call(
        functools.partial(near_kernel, sizes),
        [((team, 8, rows // 2), f32), ((half, width), bf16), ((half, both), f32)],
        (own, oth, near, heft, sums, nrow),
        [score],
        16,
        flops,
    )
    got = exchange(msg, TEAM)
    info, loss, cw = call(
        functools.partial(totals_kernel, sizes),
        [((4, rows), f32), ((1, rows), f32), ((2 * chunks, 1, 2 * piece), f32)],
        (got, heft),
    )
    cw = exchange(cw, OWNERS)
    (grads,) = call(
        functools.partial(backward_kernel, sizes),
        [((team, piece, width), bf16)],
        (own, oth, ncol_far, ncol_near, e_far, e_near, info, cw),
        [pltpu.VMEM((2, half, both), bf16), pltpu.VMEM((width, both), f32)],
        16,
        2 * flops,
    )
    shares = exchange(grads, TEAM)
    share = jnp.sum(shares.astype(f32), axis=0).astype(bf16)
    got = exchange(jnp.broadcast_to(share[None], (members, piece, width)), MP)
    grad, loss = pl.pallas_call(
        finish_kernel,
        name="finish",
        in_specs=[pl.BlockSpec(memory_space=pltpu.VMEM)] * 2,
        out_specs=[pl.BlockSpec(memory_space=pltpu.HBM)] * 2,
        out_shape=[
            jax.ShapeDtypeStruct((rows, width), f32),
            jax.ShapeDtypeStruct((1, rows), f32),
        ],
        scratch_shapes=[pltpu.VMEM((rows, width), f32), pltpu.SemaphoreType.DMA((members + 1,))],
        compiler_params=pltpu.CompilerParams(vmem_limit_bytes=4 << 20),
    )(got, loss)
    return loss.reshape(rows), grad


def solution(mesh):
    dims = {"zh": 4, "zl": 2, "yh": 4, "core": 2, "yl": 2, "x": 4}
    finer = Mesh(mesh.devices.reshape(tuple(dims.values())), tuple(dims))
    sizes = {**dims, "mp": dims["yl"] * dims["x"]}
    placed = (P(DP, None), P(DP), P(DP))
    return jax.shard_map(
        functools.partial(shards, sizes),
        mesh=finer,
        in_specs=placed,
        out_specs=(P(DP), P(DP, None)),
        check_vma=False,
    )
```

```python
import functools

import jax
import jax.numpy as jnp
from jax import lax
from jax.experimental import pallas as pl
from jax.experimental.pallas import tpu as pltpu
from jax.sharding import Mesh
from jax.sharding import PartitionSpec as P


INV_TAU = 10.0
EPS = 1e-06
LOG2E = 1.4426950408889634

DP = ("zh", "zl", "yh", "core")
MP = ("x", "yl")
FAR = ("yh", "zh")
TEAM = ("zl", "x", "yl")
OWNERS = ("core", "yh", "zh")

BLOCK = 256
NT = (((1,), (1,)), ((), ()))


def swap(x, axis):
    return lax.ppermute(x, axis, [(0, 1), (1, 0)])


def exchange(x, axes):
    return lax.all_to_all(x, axes, 0, 0, tiled=True)


def scaled(x):
    floats = x.astype(jnp.float32)
    length = jnp.sqrt(jnp.sum(floats * floats, axis=1, keepdims=True) + EPS)
    return floats, length, 1.0 / length


def place():
    zh, zl, yh, core = (lax.axis_index(a) for a in DP)
    return zh, zl, yh, core, lax.axis_index(MP)


def chunk_scalars(at, q, near, piece, sizes):
    zh, zl, yh, core, slot = at
    its_core = 1 - core if near else core
    its_yh, its_zh = q // sizes["zh"], q % sizes["zh"]
    group = ((its_zh * sizes["zl"] + zl) * sizes["yh"] + its_yh) * sizes["core"] + its_core
    base = (group * sizes["mp"] + slot) * piece
    if near:
        return base, None
    mine = jnp.logical_and(yh == its_yh, zh == its_zh)
    return base, jnp.where(mine, slot * piece, -(1 << 20))


def partner_ids(own_ref, oth_ref, rows):
    ids = []
    for ref in (own_ref, oth_ref):
        pair = ref[pl.ds(rows, 8), :].astype(jnp.float32)
        pair = (pair[0:2] * 256.0 + pair[2:4]).astype(jnp.int32)
        ids += [pair[n : n + 1] for n in range(pair.shape[0])]
    return jnp.concatenate(ids, axis=1)


def pack_kernel(views, part, weight, own, spread, heft, mates, arrived):
    rows = views.shape[0]
    piece = spread.shape[1]
    copy = pltpu.make_async_copy(views, own.at[pl.ds(0, rows)], arrived.at[0])
    small = pltpu.make_async_copy(part, mates, arrived.at[1])
    last = pltpu.make_async_copy(weight, heft, arrived.at[2])
    small.start()
    copy.start()
    last.start()
    small.wait()
    ids = mates[...]
    half_row = rows // 2
    parts = [x[:, n * half_row : (n + 1) * half_row] for x in (ids >> 8, ids & 255) for n in (0, 1)]
    blank = jnp.zeros((own.shape[0] - rows - 4, half_row), jnp.int32)
    packed = jnp.concatenate(parts + [blank], axis=0).astype(jnp.float32)
    own[pl.ds(rows, own.shape[0] - rows), :] = packed.astype(jnp.bfloat16)
    slot = lax.axis_index(MP)
    copy.wait()
    last.wait()
    mine = own[pl.ds(pl.multiple_of(slot * piece, piece), piece), :]
    for n in range(spread.shape[0]):
        spread[n] = mine


def forward_half(sizes, at, near, source, ids, nrow, ncol, e_out, s_buf, total, positive):
    chunks, piece = source.shape[0], source.shape[1]
    both = nrow.shape[0]
    rows = both // 2
    for q in range(chunks):
        floats, _, inverse = scaled(source[q])
        ncol[pl.ds(q * piece, piece), :] = (floats * inverse).astype(jnp.bfloat16)
    step = 8
    sub = lax.broadcasted_iota(jnp.int32, (step, both), 0)
    mates = jnp.broadcast_to(ids, (step, both)) - sub
    if not near:
        diag = lax.broadcasted_iota(jnp.int32, (step, rows), 1) - sub[:, :rows]
    right = nrow[...]
    for b in range(chunks * piece // BLOCK):
        s_buf[b % 2] = lax.dot_general(
            ncol[pl.ds(b * BLOCK, BLOCK), :], right, NT, preferred_element_type=jnp.float32
        )
        for c in range(BLOCK // piece):
            base, mine = chunk_scalars(at, b * (BLOCK // piece) + c, near, piece, sizes)
            for r in range(0, piece, step):
                s = s_buf[b % 2, pl.ds(c * piece + r, step), :]
                e = jnp.exp2(s * (INV_TAU * LOG2E))
                if mine is not None:
                    first = jnp.where(diag == mine + r, 0.0, e[:, :rows])
                    e = jnp.concatenate([first, e[:, rows:]], axis=1)
                e_out[pl.ds(b * BLOCK + c * piece + r, step), :] = e
                total = total + e
                positive = jnp.where(mates == base + r, s, positive)
    return total, positive


def rows_kernel(own, oth, nrow, ids):
    rows = nrow.shape[0] // 2
    for at, source in ((0, own[0:rows, :]), (rows, oth[0:rows, :])):
        floats, _, inverse = scaled(source)
        nrow[pl.ds(at, rows), :] = (floats * inverse).astype(jnp.bfloat16)
    ids[...] = partner_ids(own, oth, rows)


def far_kernel(sizes, far, ids, nrow, sums, ncol, e_out, s_buf):
    zero = jnp.zeros((8, nrow.shape[0]), jnp.float32)
    total, positive = forward_half(
        sizes, place(), False, far, ids[...], nrow, ncol, e_out, s_buf, zero, zero
    )
    sums[0] = total
    sums[1] = positive


def near_kernel(sizes, near, ids, weight, sums, nrow, msg, ncol, e_out, s_buf):
    rows = nrow.shape[0] // 2
    at = place()
    total, positive = forward_half(
        sizes, at, True, near, ids[...], nrow, ncol, e_out, s_buf, sums[0], sums[1]
    )
    total = jnp.sum(total, axis=0, keepdims=True)
    positive = jnp.sum(positive, axis=0, keepdims=True) * INV_TAU
    zl = at[1]
    same = [total[:, :rows], total[:, rows:], positive[:, :rows], weight[...]]
    turned = [total[:, rows:], total[:, :rows], positive[:, rows:], weight[...]]
    half_row = rows // 2

    def stacked(parts):
        return jnp.concatenate(
            [p[:, n * half_row : (n + 1) * half_row] for p in parts for n in range(2)], axis=0
        )

    same, turned = stacked(same), stacked(turned)
    members = sizes["mp"]
    for n in range(members):
        msg[zl * members + n] = same
        msg[(1 - zl) * members + n] = turned


def totals_kernel(sizes, got, weight, info, loss, cw):
    _, zl, _, _, slot = place()
    members = sizes["mp"]
    summed = got[0]
    for n in range(1, got.shape[0]):
        summed = summed + got[n]
    other_weight = got[(1 - zl) * members, 6:8, :]

    def joined(pair):
        return jnp.concatenate([pair[0:1], pair[1:2]], axis=1)

    total, total_other = joined(summed[0:2]), joined(summed[2:4])
    positive = joined(summed[4:6])
    other_weight = joined(other_weight)
    own_weight = weight[...]
    share = own_weight / total
    share_other = other_weight / total_other
    loss[...] = jnp.log(total) - positive
    info[...] = jnp.concatenate([share, share_other, own_weight, other_weight], axis=0)
    piece = own_weight.shape[1] // members
    out = jnp.zeros((1, 2 * piece), jnp.float32)
    for n in range(members):
        at = slice(n * piece, (n + 1) * piece)
        out = jnp.where(slot == n, jnp.concatenate([share[:, at], own_weight[:, at]], axis=1), out)
    for n in range(cw.shape[0]):
        cw[n] = out


def backward_kernel(
    sizes, own, oth, ids, ncol_far, ncol_near, e_far, e_near, info, cw, msg, coef, acc
):
    both, width = acc.shape[1], acc.shape[0]
    rows = both // 2
    chunks = cw.shape[0] // 2
    half = ncol_far.shape[0]
    piece = half // chunks
    step = 16
    at = place()
    mates = jnp.broadcast_to(ids[...], (step, both)) - lax.broadcasted_iota(jnp.int32, (step, both), 0)
    row_share = jnp.concatenate([info[0:1, :], info[1:2, :]], axis=1)
    row_weight = jnp.concatenate([info[2:3, :], info[3:4, :]], axis=1)
    row_share = jnp.broadcast_to(row_share, (step, both))
    row_weight = jnp.broadcast_to(row_weight, (step, both))
    turn = 0
    for near, ncol, e_ref in ((False, ncol_far, e_far), (True, ncol_near, e_near)):
        core = 1 - at[3] if near else at[3]
        columns = cw[pl.ds(core * chunks, chunks)].reshape(chunks, 2 * piece).T
        for b in range(half // BLOCK):
            for c in range(BLOCK // piece):
                q = b * (BLOCK // piece) + c
                base, _ = chunk_scalars(at, q, near, piece, sizes)
                column = columns[:, q : q + 1]
                for r in range(0, piece, step):
                    e = e_ref[pl.ds(b * BLOCK + c * piece + r, step), :]
                    value = e * (row_share + column[r : r + step])
                    pull = row_weight + column[piece + r : piece + r + step]
                    value = jnp.where(mates == base + r, value - pull, value)
                    coef[turn, pl.ds(b * BLOCK + c * piece + r, step), :] = value.astype(jnp.bfloat16)
        product = jnp.dot(ncol[...].T, coef[turn], preferred_element_type=jnp.float32)
        if turn == 0:
            acc[...] = product
        else:
            acc[...] += product
        turn += 1
    zl = at[1]
    members = sizes["mp"]
    for to, first, source in ((zl, 0, own[0:rows, :]), (1 - zl, rows, oth[0:rows, :])):
        floats, _, inverse = scaled(source)
        g = acc[:, first : first + rows].T * INV_TAU
        unit = floats * inverse
        out = (g - unit * jnp.sum(unit * g, axis=1, keepdims=True)) * inverse
        msg[pl.ds(to * members, members)] = out.astype(jnp.bfloat16).reshape(members, -1, width)


def finish_kernel(got, loss, out, loss_out, wide, stored):
    piece = got.shape[1]
    copies = [pltpu.make_async_copy(loss, loss_out, stored.at[got.shape[0]])]
    copies[0].start()
    for n in range(got.shape[0]):
        at = pl.ds(n * piece, piece)
        wide[at, :] = got[n].astype(jnp.float32)
        copies.append(pltpu.make_async_copy(wide.at[at], out.at[at], stored.at[n]))
        copies[-1].start()
    for copy in copies:
        copy.wait()


def call(kernel, outs, args, scratch=(), mib=4, flops=0):
    vmem = pl.BlockSpec(memory_space=pltpu.VMEM)
    return pl.pallas_call(
        kernel,
        in_specs=[vmem] * len(args),
        out_specs=[vmem] * len(outs),
        out_shape=[jax.ShapeDtypeStruct(*o) for o in outs],
        scratch_shapes=list(scratch),
        compiler_params=pltpu.CompilerParams(vmem_limit_bytes=mib << 20),
        cost_estimate=pl.CostEstimate(flops=flops, bytes_accessed=1 << 20, transcendentals=0),
    )(*args)


def shards(sizes, views, partner, weight):
    return body(sizes, views, partner, weight)


def body(sizes, views, partner, weight):
    rows, width = views.shape
    members = sizes["mp"]
    piece = rows // members
    f32, bf16 = jnp.float32, jnp.bfloat16

    chunks = sizes["zh"] * sizes["yh"]
    own, spread, heft = pl.pallas_call(
        pack_kernel,
        name="pack",
        in_specs=[pl.BlockSpec(memory_space=pltpu.HBM)] * 3,
        out_specs=[pl.BlockSpec(memory_space=pltpu.VMEM)] * 3,
        out_shape=[
            jax.ShapeDtypeStruct((rows + 16, width), bf16),
            jax.ShapeDtypeStruct((chunks, piece, width), bf16),
            jax.ShapeDtypeStruct((1, rows), f32),
        ],
        scratch_shapes=[pltpu.VMEM((1, rows), jnp.int32), pltpu.SemaphoreType.DMA((3,))],
        compiler_params=pltpu.CompilerParams(vmem_limit_bytes=4 << 20),
    )(*[
        pltpu.with_memory_space_constraint(a, pltpu.HBM)
        for a in (views, partner.reshape(1, rows), weight.reshape(1, rows))
    ])
    oth = swap(own, "zl")
    far = exchange(spread, FAR)
    both = 2 * rows
    nrow, ids = call(rows_kernel, [((both, width), bf16), ((1, both), jnp.int32)], (own, oth))
    near = swap(far, "core")

    half, team = chunks * piece, 2 * members
    flops = 2 * half * both * width
    score = pltpu.VMEM((2, BLOCK, both), f32)
    sums, ncol_far, e_far = call(
        functools.partial(far_kernel, sizes),
        [((2, 8, both), f32), ((half, width), bf16), ((half, both), f32)],
        (far, ids, nrow),
        [score],
        16,
        flops,
    )
    msg, ncol_near, e_near = call(
        functools.partial(near_kernel, sizes),
        [((team, 8, rows // 2), f32), ((half, width), bf16), ((half, both), f32)],
        (near, ids, heft, sums, nrow),
        [score],
        16,
        flops,
    )
    got = exchange(msg, TEAM)
    info, loss, cw = call(
        functools.partial(totals_kernel, sizes),
        [((4, rows), f32), ((1, rows), f32), ((2 * chunks, 1, 2 * piece), f32)],
        (got, heft),
    )
    cw = exchange(cw, OWNERS)
    (grads,) = call(
        functools.partial(backward_kernel, sizes),
        [((team, piece, width), bf16)],
        (own, oth, ids, ncol_far, ncol_near, e_far, e_near, info, cw),
        [pltpu.VMEM((2, half, both), bf16), pltpu.VMEM((width, both), f32)],
        16,
        2 * flops,
    )
    shares = exchange(grads, TEAM)
    share = jnp.sum(shares.astype(f32), axis=0).astype(bf16)
    got = exchange(jnp.broadcast_to(share[None], (members, piece, width)), MP)
    grad, loss = pl.pallas_call(
        finish_kernel,
        name="finish",
        in_specs=[pl.BlockSpec(memory_space=pltpu.VMEM)] * 2,
        out_specs=[pl.BlockSpec(memory_space=pltpu.HBM)] * 2,
        out_shape=[
            jax.ShapeDtypeStruct((rows, width), f32),
            jax.ShapeDtypeStruct((1, rows), f32),
        ],
        scratch_shapes=[pltpu.VMEM((rows, width), f32), pltpu.SemaphoreType.DMA((members + 1,))],
        compiler_params=pltpu.CompilerParams(vmem_limit_bytes=4 << 20),
    )(got, loss)
    return loss.reshape(rows), grad


def solution(mesh):
    dims = {"zh": 4, "zl": 2, "yh": 4, "core": 2, "yl": 2, "x": 4}
    finer = Mesh(mesh.devices.reshape(tuple(dims.values())), tuple(dims))
    sizes = {**dims, "mp": dims["yl"] * dims["x"]}
    placed = (P(DP, None), P(DP), P(DP))
    return jax.shard_map(
        functools.partial(shards, sizes),
        mesh=finer,
        in_specs=placed,
        out_specs=(P(DP), P(DP, None)),
        check_vma=False,
    )
```

```python
import functools

import jax
import jax.numpy as jnp
from jax import lax
from jax.experimental import pallas as pl
from jax.experimental.pallas import tpu as pltpu
from jax.sharding import Mesh
from jax.sharding import PartitionSpec as P


INV_TAU = 10.0
EPS = 1e-06
LOG2E = 1.4426950408889634

DP = ("zh", "zl", "yh", "core")
MP = ("x", "yl")
FAR = ("yh", "zh")
TEAM = ("zl", "x", "yl")
OWNERS = ("core", "yh", "zh")

BLOCK = 256
NT = (((1,), (1,)), ((), ()))


def swap(x, axis):
    return lax.ppermute(x, axis, [(0, 1), (1, 0)])


def exchange(x, axes):
    return lax.all_to_all(x, axes, 0, 0, tiled=True)


def scaled(x):
    floats = x.astype(jnp.float32)
    length = jnp.sqrt(jnp.sum(floats * floats, axis=1, keepdims=True) + EPS)
    return floats, length, 1.0 / length


def place():
    zh, zl, yh, core = (lax.axis_index(a) for a in DP)
    return zh, zl, yh, core, lax.axis_index(MP)


def chunk_scalars(at, q, near, piece, sizes):
    zh, zl, yh, core, slot = at
    its_core = 1 - core if near else core
    its_yh, its_zh = q // sizes["zh"], q % sizes["zh"]
    group = ((its_zh * sizes["zl"] + zl) * sizes["yh"] + its_yh) * sizes["core"] + its_core
    base = (group * sizes["mp"] + slot) * piece
    if near:
        return base, None
    mine = jnp.logical_and(yh == its_yh, zh == its_zh)
    return base, jnp.where(mine, slot * piece, -(1 << 20))


def triple(x):
    high = x.astype(jnp.bfloat16).astype(jnp.float32)
    rest = x - high
    middle = rest.astype(jnp.bfloat16).astype(jnp.float32)
    return high, middle, rest - middle


def row_weights(refs, rows):
    parts = []
    for ref in refs:
        tail = ref[pl.ds(rows, 16), :].astype(jnp.float32)
        pair = tail[4:6] + tail[6:8] + tail[8:10]
        parts += [pair[n : n + 1] for n in range(pair.shape[0])]
    return jnp.concatenate(parts, axis=1)


def partner_ids(own_ref, oth_ref, rows):
    ids = []
    for ref in (own_ref, oth_ref):
        pair = ref[pl.ds(rows, 8), :].astype(jnp.float32)
        pair = (pair[0:2] * 256.0 + pair[2:4]).astype(jnp.int32)
        ids += [pair[n : n + 1] for n in range(pair.shape[0])]
    return jnp.concatenate(ids, axis=1)


def pack_kernel(views, part, weight, own, spread, heft, mates, arrived):
    rows = views.shape[0]
    piece = spread.shape[1]
    copy = pltpu.make_async_copy(views, own.at[pl.ds(0, rows)], arrived.at[0])
    small = pltpu.make_async_copy(part, mates, arrived.at[1])
    last = pltpu.make_async_copy(weight, heft, arrived.at[2])
    small.start()
    copy.start()
    last.start()
    small.wait()
    ids = mates[...]
    half_row = rows // 2
    parts = [x[:, n * half_row : (n + 1) * half_row] for x in (ids >> 8, ids & 255) for n in (0, 1)]
    parts = [x.astype(jnp.float32) for x in parts]
    last.wait()
    for x in triple(heft[...]):
        parts += [x[:, n * half_row : (n + 1) * half_row] for n in (0, 1)]
    parts.append(jnp.zeros((own.shape[0] - rows - len(parts), half_row), jnp.float32))
    packed = jnp.concatenate(parts, axis=0)
    own[pl.ds(rows, own.shape[0] - rows), :] = packed.astype(jnp.bfloat16)
    slot = lax.axis_index(MP)
    copy.wait()
    mine = own[pl.ds(pl.multiple_of(slot * piece, piece), piece), :]
    for n in range(spread.shape[0]):
        spread[n] = mine


def forward_half(sizes, at, near, source, ids, nrow, ncol, e_out, s_buf, total, positive):
    chunks, piece = source.shape[0], source.shape[1]
    both = nrow.shape[0]
    rows = both // 2
    for q in range(chunks):
        floats, _, inverse = scaled(source[q])
        ncol[pl.ds(q * piece, piece), :] = (floats * inverse).astype(jnp.bfloat16)
    step = 8
    sub = lax.broadcasted_iota(jnp.int32, (step, both), 0)
    mates = jnp.broadcast_to(ids, (step, both)) - sub
    if not near:
        diag = lax.broadcasted_iota(jnp.int32, (step, rows), 1) - sub[:, :rows]
    right = nrow[...]
    for b in range(chunks * piece // BLOCK):
        s_buf[b % 2] = lax.dot_general(
            ncol[pl.ds(b * BLOCK, BLOCK), :], right, NT, preferred_element_type=jnp.float32
        )
        for c in range(BLOCK // piece):
            base, mine = chunk_scalars(at, b * (BLOCK // piece) + c, near, piece, sizes)
            for r in range(0, piece, step):
                s = s_buf[b % 2, pl.ds(c * piece + r, step), :]
                e = jnp.exp2(s * (INV_TAU * LOG2E))
                if mine is not None:
                    first = jnp.where(diag == mine + r, 0.0, e[:, :rows])
                    e = jnp.concatenate([first, e[:, rows:]], axis=1)
                e_out[pl.ds(b * BLOCK + c * piece + r, step), :] = e
                total = total + e
                positive = jnp.where(mates == base + r, s, positive)
    return total, positive


def far_kernel(sizes, own, oth, far, sums, ncol, nrow, e_out, s_buf):
    rows = nrow.shape[0] // 2
    for at, source in ((0, own[0:rows, :]), (rows, oth[0:rows, :])):
        floats, _, inverse = scaled(source)
        nrow[pl.ds(at, rows), :] = (floats * inverse).astype(jnp.bfloat16)
    ids = partner_ids(own, oth, rows)
    zero = jnp.zeros((8, 2 * rows), jnp.float32)
    total, positive = forward_half(
        sizes, place(), False, far, ids, nrow, ncol, e_out, s_buf, zero, zero
    )
    sums[0] = total
    sums[1] = positive


def near_kernel(sizes, own, oth, near, sums, nrow, msg, ncol, e_out, s_buf):
    rows = nrow.shape[0] // 2
    at = place()
    ids = partner_ids(own, oth, rows)
    total, positive = forward_half(
        sizes, at, True, near, ids, nrow, ncol, e_out, s_buf, sums[0], sums[1]
    )
    total = jnp.sum(total, axis=0, keepdims=True)
    positive = jnp.sum(positive, axis=0, keepdims=True) * INV_TAU
    zl = at[1]
    same = jnp.concatenate([total[:, :rows], total[:, rows:], positive[:, :rows]], axis=1)
    turned = jnp.concatenate([total[:, rows:], total[:, :rows], positive[:, rows:]], axis=1)
    members = sizes["mp"]
    for n in range(members):
        msg[zl * members + n] = same
        msg[(1 - zl) * members + n] = turned


def totals_kernel(sizes, oth, got, weight, info, loss, cw):
    slot = place()[4]
    members = sizes["mp"]
    summed = got[0]
    for n in range(1, got.shape[0]):
        summed = summed + got[n]
    rows = weight.shape[1]
    total, total_other = summed[:, :rows], summed[:, rows : 2 * rows]
    positive = summed[:, 2 * rows :]
    own_weight, other_weight = weight[...], row_weights((oth,), rows)
    share = own_weight / total
    share_other = other_weight / total_other
    loss[...] = jnp.log(total) - positive
    info[...] = jnp.concatenate([share, share_other, own_weight, other_weight], axis=0)
    piece = own_weight.shape[1] // members
    out = jnp.zeros((1, 2 * piece), jnp.float32)
    for n in range(members):
        at = slice(n * piece, (n + 1) * piece)
        out = jnp.where(slot == n, jnp.concatenate([share[:, at], own_weight[:, at]], axis=1), out)
    for n in range(cw.shape[0]):
        cw[n] = out


def backward_kernel(
    sizes, own, oth, ncol_far, ncol_near, e_far, e_near, info, cw, msg, coef, acc
):
    both, width = acc.shape[1], acc.shape[0]
    rows = both // 2
    chunks = cw.shape[0] // 2
    half = ncol_far.shape[0]
    piece = half // chunks
    step = 16
    at = place()
    ids = partner_ids(own, oth, rows)
    mates = jnp.broadcast_to(ids, (step, both)) - lax.broadcasted_iota(jnp.int32, (step, both), 0)
    row_share = jnp.concatenate([info[0:1, :], info[1:2, :]], axis=1)
    row_weight = jnp.concatenate([info[2:3, :], info[3:4, :]], axis=1)
    row_share = jnp.broadcast_to(row_share, (step, both))
    row_weight = jnp.broadcast_to(row_weight, (step, both))
    turn = 0
    for near, ncol, e_ref in ((False, ncol_far, e_far), (True, ncol_near, e_near)):
        core = 1 - at[3] if near else at[3]
        columns = cw[pl.ds(core * chunks, chunks)].reshape(chunks, 2 * piece).T
        for b in range(half // BLOCK):
            for c in range(BLOCK // piece):
                q = b * (BLOCK // piece) + c
                base, _ = chunk_scalars(at, q, near, piece, sizes)
                column = columns[:, q : q + 1]
                for r in range(0, piece, step):
                    e = e_ref[pl.ds(b * BLOCK + c * piece + r, step), :]
                    value = e * (row_share + column[r : r + step])
                    pull = row_weight + column[piece + r : piece + r + step]
                    value = jnp.where(mates == base + r, value - pull, value)
                    coef[turn, pl.ds(b * BLOCK + c * piece + r, step), :] = value.astype(jnp.bfloat16)
        product = jnp.dot(ncol[...].T, coef[turn], preferred_element_type=jnp.float32)
        if turn == 0:
            acc[...] = product
        else:
            acc[...] += product
        turn += 1
    zl = at[1]
    members = sizes["mp"]
    for to, first, source in ((zl, 0, own[0:rows, :]), (1 - zl, rows, oth[0:rows, :])):
        floats, _, inverse = scaled(source)
        g = acc[:, first : first + rows].T * INV_TAU
        unit = floats * inverse
        out = (g - unit * jnp.sum(unit * g, axis=1, keepdims=True)) * inverse
        msg[pl.ds(to * members, members)] = out.astype(jnp.bfloat16).reshape(members, -1, width)


def finish_kernel(got, loss, out, loss_out, wide, stored):
    piece = got.shape[1]
    copies = [pltpu.make_async_copy(loss, loss_out, stored.at[got.shape[0]])]
    copies[0].start()
    for n in range(got.shape[0]):
        at = pl.ds(n * piece, piece)
        wide[at, :] = got[n].astype(jnp.float32)
        copies.append(pltpu.make_async_copy(wide.at[at], out.at[at], stored.at[n]))
        copies[-1].start()
    for copy in copies:
        copy.wait()


def call(kernel, outs, args, scratch=(), mib=4, flops=0):
    vmem = pl.BlockSpec(memory_space=pltpu.VMEM)
    return pl.pallas_call(
        kernel,
        in_specs=[vmem] * len(args),
        out_specs=[vmem] * len(outs),
        out_shape=[jax.ShapeDtypeStruct(*o) for o in outs],
        scratch_shapes=list(scratch),
        compiler_params=pltpu.CompilerParams(vmem_limit_bytes=mib << 20),
        cost_estimate=pl.CostEstimate(flops=flops, bytes_accessed=1 << 20, transcendentals=0),
    )(*args)


def shards(sizes, views, partner, weight):
    return body(sizes, views, partner, weight)


def body(sizes, views, partner, weight):
    rows, width = views.shape
    members = sizes["mp"]
    piece = rows // members
    f32, bf16 = jnp.float32, jnp.bfloat16

    chunks = sizes["zh"] * sizes["yh"]
    own, spread, heft = pl.pallas_call(
        pack_kernel,
        name="pack",
        in_specs=[pl.BlockSpec(memory_space=pltpu.HBM)] * 3,
        out_specs=[pl.BlockSpec(memory_space=pltpu.VMEM)] * 3,
        out_shape=[
            jax.ShapeDtypeStruct((rows + 16, width), bf16),
            jax.ShapeDtypeStruct((chunks, piece, width), bf16),
            jax.ShapeDtypeStruct((1, rows), f32),
        ],
        scratch_shapes=[pltpu.VMEM((1, rows), jnp.int32), pltpu.SemaphoreType.DMA((3,))],
        compiler_params=pltpu.CompilerParams(vmem_limit_bytes=4 << 20),
    )(*[
        pltpu.with_memory_space_constraint(a, pltpu.HBM)
        for a in (views, partner.reshape(1, rows), weight.reshape(1, rows))
    ])
    oth = swap(own, "zl")
    far = exchange(spread, FAR)
    near = swap(far, "core")

    half, both, team = chunks * piece, 2 * rows, 2 * members
    flops = 2 * half * both * width
    score = pltpu.VMEM((2, BLOCK, both), f32)
    sums, ncol_far, nrow, e_far = call(
        functools.partial(far_kernel, sizes),
        [((2, 8, both), f32), ((half, width), bf16), ((both, width), bf16), ((half, both), f32)],
        (own, oth, far),
        [score],
        16,
        flops,
    )
    msg, ncol_near, e_near = call(
        functools.partial(near_kernel, sizes),
        [((team, 1, 3 * rows), f32), ((half, width), bf16), ((half, both), f32)],
        (own, oth, near, sums, nrow),
        [score],
        16,
        flops,
    )
    got = exchange(msg, TEAM)
    info, loss, cw = call(
        functools.partial(totals_kernel, sizes),
        [((4, rows), f32), ((1, rows), f32), ((2 * chunks, 1, 2 * piece), f32)],
        (oth, got, heft),
    )
    cw = exchange(cw, OWNERS)
    (grads,) = call(
        functools.partial(backward_kernel, sizes),
        [((team, piece, width), bf16)],
        (own, oth, ncol_far, ncol_near, e_far, e_near, info, cw),
        [pltpu.VMEM((2, half, both), bf16), pltpu.VMEM((width, both), f32)],
        16,
        2 * flops,
    )
    shares = exchange(grads, TEAM)
    share = jnp.sum(shares.astype(f32), axis=0).astype(bf16)
    got = exchange(jnp.broadcast_to(share[None], (members, piece, width)), MP)
    grad, loss = pl.pallas_call(
        finish_kernel,
        name="finish",
        in_specs=[pl.BlockSpec(memory_space=pltpu.VMEM)] * 2,
        out_specs=[pl.BlockSpec(memory_space=pltpu.HBM)] * 2,
        out_shape=[
            jax.ShapeDtypeStruct((rows, width), f32),
            jax.ShapeDtypeStruct((1, rows), f32),
        ],
        scratch_shapes=[pltpu.VMEM((rows, width), f32), pltpu.SemaphoreType.DMA((members + 1,))],
        compiler_params=pltpu.CompilerParams(vmem_limit_bytes=4 << 20),
    )(got, loss)
    return loss.reshape(rows), grad


def solution(mesh):
    dims = {"zh": 4, "zl": 2, "yh": 4, "core": 2, "yl": 2, "x": 4}
    finer = Mesh(mesh.devices.reshape(tuple(dims.values())), tuple(dims))
    sizes = {**dims, "mp": dims["yl"] * dims["x"]}
    placed = (P(DP, None), P(DP), P(DP))
    return jax.shard_map(
        functools.partial(shards, sizes),
        mesh=finer,
        in_specs=placed,
        out_specs=(P(DP), P(DP, None)),
        check_vma=False,
    )
```

```python
import functools

import jax
import jax.numpy as jnp
from jax import lax
from jax.experimental import pallas as pl
from jax.experimental.pallas import tpu as pltpu
from jax.sharding import Mesh
from jax.sharding import PartitionSpec as P


INV_TAU = 10.0
EPS = 1e-06
LOG2E = 1.4426950408889634

DP = ("zh", "zl", "yh", "core")
MP = ("x", "yl")
FAR = ("yh", "zh")
TEAM = ("zl", "x", "yl")
OWNERS = ("core", "yh", "zh")

BLOCK = 256
NT = (((1,), (1,)), ((), ()))


def swap(x, axis):
    return lax.ppermute(x, axis, [(0, 1), (1, 0)])


def exchange(x, axes):
    return lax.all_to_all(x, axes, 0, 0, tiled=True)


def scaled(x):
    floats = x.astype(jnp.float32)
    length = jnp.sqrt(jnp.sum(floats * floats, axis=1, keepdims=True) + EPS)
    return floats, length, 1.0 / length


def place():
    zh, zl, yh, core = (lax.axis_index(a) for a in DP)
    return zh, zl, yh, core, lax.axis_index(MP)


def chunk_scalars(at, q, near, piece, sizes):
    zh, zl, yh, core, slot = at
    its_core = 1 - core if near else core
    its_yh, its_zh = q // sizes["zh"], q % sizes["zh"]
    group = ((its_zh * sizes["zl"] + zl) * sizes["yh"] + its_yh) * sizes["core"] + its_core
    base = (group * sizes["mp"] + slot) * piece
    if near:
        return base, None
    mine = jnp.logical_and(yh == its_yh, zh == its_zh)
    return base, jnp.where(mine, slot * piece, -(1 << 20))


def triple(x):
    high = x.astype(jnp.bfloat16).astype(jnp.float32)
    rest = x - high
    middle = rest.astype(jnp.bfloat16).astype(jnp.float32)
    return high, middle, rest - middle


def row_weights(refs, rows):
    parts = []
    for ref in refs:
        tail = ref[pl.ds(rows, 16), :].astype(jnp.float32)
        pair = tail[4:6] + tail[6:8] + tail[8:10]
        parts += [pair[n : n + 1] for n in range(pair.shape[0])]
    return jnp.concatenate(parts, axis=1)


def partner_ids(own_ref, oth_ref, rows):
    ids = []
    for ref in (own_ref, oth_ref):
        pair = ref[pl.ds(rows, 8), :].astype(jnp.float32)
        pair = (pair[0:2] * 256.0 + pair[2:4]).astype(jnp.int32)
        ids += [pair[n : n + 1] for n in range(pair.shape[0])]
    return jnp.concatenate(ids, axis=1)


def pack_kernel(views, part, weight, own, spread, heft, mates, arrived):
    rows = views.shape[0]
    piece = spread.shape[1]
    copy = pltpu.make_async_copy(views, own.at[pl.ds(0, rows)], arrived.at[0])
    small = pltpu.make_async_copy(part, mates, arrived.at[1])
    last = pltpu.make_async_copy(weight, heft, arrived.at[2])
    small.start()
    copy.start()
    last.start()
    small.wait()
    ids = mates[...]
    half_row = rows // 2
    parts = [x[:, n * half_row : (n + 1) * half_row] for x in (ids >> 8, ids & 255) for n in (0, 1)]
    parts = [x.astype(jnp.float32) for x in parts]
    last.wait()
    for x in triple(heft[...]):
        parts += [x[:, n * half_row : (n + 1) * half_row] for n in (0, 1)]
    parts.append(jnp.zeros((own.shape[0] - rows - len(parts), half_row), jnp.float32))
    packed = jnp.concatenate(parts, axis=0)
    own[pl.ds(rows, own.shape[0] - rows), :] = packed.astype(jnp.bfloat16)
    slot = lax.axis_index(MP)
    copy.wait()
    mine = own[pl.ds(pl.multiple_of(slot * piece, piece), piece), :]
    for n in range(spread.shape[0]):
        spread[n] = mine


def forward_half(sizes, at, near, source, ids, nrow, ncol, e_out, s_buf, total, positive):
    chunks, piece = source.shape[0], source.shape[1]
    both = nrow.shape[0]
    rows = both // 2
    for q in range(chunks):
        floats, _, inverse = scaled(source[q])
        ncol[pl.ds(q * piece, piece), :] = (floats * inverse).astype(jnp.bfloat16)
    step = 8
    sub = lax.broadcasted_iota(jnp.int32, (step, both), 0)
    mates = jnp.broadcast_to(ids, (step, both)) - sub
    if not near:
        diag = lax.broadcasted_iota(jnp.int32, (step, rows), 1) - sub[:, :rows]
    right = nrow[...]
    for b in range(chunks * piece // BLOCK):
        s_buf[b % 2] = lax.dot_general(
            ncol[pl.ds(b * BLOCK, BLOCK), :], right, NT, preferred_element_type=jnp.float32
        )
        for c in range(BLOCK // piece):
            base, mine = chunk_scalars(at, b * (BLOCK // piece) + c, near, piece, sizes)
            for r in range(0, piece, step):
                s = s_buf[b % 2, pl.ds(c * piece + r, step), :]
                e = jnp.exp2(s * (INV_TAU * LOG2E))
                if mine is not None:
                    first = jnp.where(diag == mine + r, 0.0, e[:, :rows])
                    e = jnp.concatenate([first, e[:, rows:]], axis=1)
                e_out[pl.ds(b * BLOCK + c * piece + r, step), :] = e
                total = total + e
                positive = jnp.where(mates == base + r, s, positive)
    return total, positive


def far_kernel(sizes, own, oth, far, sums, ncol, nrow, e_out, s_buf):
    rows = nrow.shape[0] // 2
    for at, source in ((0, own[0:rows, :]), (rows, oth[0:rows, :])):
        floats, _, inverse = scaled(source)
        nrow[pl.ds(at, rows), :] = (floats * inverse).astype(jnp.bfloat16)
    ids = partner_ids(own, oth, rows)
    zero = jnp.zeros((8, 2 * rows), jnp.float32)
    total, positive = forward_half(
        sizes, place(), False, far, ids, nrow, ncol, e_out, s_buf, zero, zero
    )
    sums[0] = total
    sums[1] = positive


def near_kernel(sizes, own, oth, near, sums, nrow, msg, ncol, e_out, s_buf):
    rows = nrow.shape[0] // 2
    at = place()
    ids = partner_ids(own, oth, rows)
    total, positive = forward_half(
        sizes, at, True, near, ids, nrow, ncol, e_out, s_buf, sums[0], sums[1]
    )
    total = jnp.sum(total, axis=0, keepdims=True)
    positive = jnp.sum(positive, axis=0, keepdims=True) * INV_TAU
    zl = at[1]
    same = jnp.concatenate([total[:, :rows], total[:, rows:], positive[:, :rows]], axis=1)
    turned = jnp.concatenate([total[:, rows:], total[:, :rows], positive[:, rows:]], axis=1)
    members = sizes["mp"]
    for n in range(members):
        msg[zl * members + n] = same
        msg[(1 - zl) * members + n] = turned


def totals_kernel(sizes, oth, got, weight, info, loss, cw):
    slot = place()[4]
    members = sizes["mp"]
    summed = got[0]
    for n in range(1, got.shape[0]):
        summed = summed + got[n]
    rows = weight.shape[1]
    total, total_other = summed[:, :rows], summed[:, rows : 2 * rows]
    positive = summed[:, 2 * rows :]
    own_weight, other_weight = weight[...], row_weights((oth,), rows)
    share = own_weight / total
    share_other = other_weight / total_other
    loss[...] = jnp.log(total) - positive
    info[...] = jnp.concatenate([share, share_other, own_weight, other_weight], axis=0)
    piece = own_weight.shape[1] // members
    out = jnp.zeros((1, 2 * piece), jnp.float32)
    for n in range(members):
        at = slice(n * piece, (n + 1) * piece)
        out = jnp.where(slot == n, jnp.concatenate([share[:, at], own_weight[:, at]], axis=1), out)
    for n in range(cw.shape[0]):
        cw[n] = out


def backward_kernel(
    sizes, own, oth, ncol_far, ncol_near, e_far, e_near, info, cw, msg, coef, acc
):
    both, width = acc.shape[1], acc.shape[0]
    rows = both // 2
    chunks = cw.shape[0] // 2
    half = ncol_far.shape[0]
    piece = half // chunks
    step = 16
    at = place()
    ids = partner_ids(own, oth, rows)
    mates = jnp.broadcast_to(ids, (step, both)) - lax.broadcasted_iota(jnp.int32, (step, both), 0)
    row_share = jnp.concatenate([info[0:1, :], info[1:2, :]], axis=1)
    row_weight = jnp.concatenate([info[2:3, :], info[3:4, :]], axis=1)
    row_share = jnp.broadcast_to(row_share, (step, both))
    row_weight = jnp.broadcast_to(row_weight, (step, both))
    turn = 0
    for near, ncol, e_ref in ((False, ncol_far, e_far), (True, ncol_near, e_near)):
        core = 1 - at[3] if near else at[3]
        columns = cw[pl.ds(core * chunks, chunks)].reshape(chunks, 2 * piece).T
        for b in range(half // BLOCK):
            for c in range(BLOCK // piece):
                q = b * (BLOCK // piece) + c
                base, _ = chunk_scalars(at, q, near, piece, sizes)
                column = columns[:, q : q + 1]
                for r in range(0, piece, step):
                    e = e_ref[pl.ds(b * BLOCK + c * piece + r, step), :]
                    value = e * (row_share + column[r : r + step])
                    pull = row_weight + column[piece + r : piece + r + step]
                    value = jnp.where(mates == base + r, value - pull, value)
                    coef[turn, pl.ds(b * BLOCK + c * piece + r, step), :] = value.astype(jnp.bfloat16)
        product = jnp.dot(ncol[...].T, coef[turn], preferred_element_type=jnp.float32)
        if turn == 0:
            acc[...] = product
        else:
            acc[...] += product
        turn += 1
    zl = at[1]
    members = sizes["mp"]
    for to, first, source in ((zl, 0, own[0:rows, :]), (1 - zl, rows, oth[0:rows, :])):
        floats, _, inverse = scaled(source)
        g = acc[:, first : first + rows].T * INV_TAU
        unit = floats * inverse
        out = (g - unit * jnp.sum(unit * g, axis=1, keepdims=True)) * inverse
        msg[pl.ds(to * members, members)] = out.astype(jnp.bfloat16).reshape(members, -1, width)


def owner_kernel(got, out):
    total = got[0].astype(jnp.float32)
    for n in range(1, got.shape[0]):
        total = total + got[n].astype(jnp.float32)
    total = total.astype(jnp.bfloat16)
    for n in range(out.shape[0]):
        out[n] = total


def finish_kernel(got, loss, out, loss_out, wide, stored):
    piece = got.shape[1]
    copies = [pltpu.make_async_copy(loss, loss_out, stored.at[got.shape[0]])]
    copies[0].start()
    for n in range(got.shape[0]):
        at = pl.ds(n * piece, piece)
        wide[at, :] = got[n].astype(jnp.float32)
        copies.append(pltpu.make_async_copy(wide.at[at], out.at[at], stored.at[n]))
        copies[-1].start()
    for copy in copies:
        copy.wait()


def call(kernel, outs, args, scratch=(), mib=4, flops=0):
    vmem = pl.BlockSpec(memory_space=pltpu.VMEM)
    return pl.pallas_call(
        kernel,
        in_specs=[vmem] * len(args),
        out_specs=[vmem] * len(outs),
        out_shape=[jax.ShapeDtypeStruct(*o) for o in outs],
        scratch_shapes=list(scratch),
        compiler_params=pltpu.CompilerParams(vmem_limit_bytes=mib << 20),
        cost_estimate=pl.CostEstimate(flops=flops, bytes_accessed=1 << 20, transcendentals=0),
    )(*args)


def shards(sizes, views, partner, weight):
    return body(sizes, views, partner, weight)


def body(sizes, views, partner, weight):
    rows, width = views.shape
    members = sizes["mp"]
    piece = rows // members
    f32, bf16 = jnp.float32, jnp.bfloat16

    chunks = sizes["zh"] * sizes["yh"]
    own, spread, heft = pl.pallas_call(
        pack_kernel,
        name="pack",
        in_specs=[pl.BlockSpec(memory_space=pltpu.HBM)] * 3,
        out_specs=[pl.BlockSpec(memory_space=pltpu.VMEM)] * 3,
        out_shape=[
            jax.ShapeDtypeStruct((rows + 16, width), bf16),
            jax.ShapeDtypeStruct((chunks, piece, width), bf16),
            jax.ShapeDtypeStruct((1, rows), f32),
        ],
        scratch_shapes=[pltpu.VMEM((1, rows), jnp.int32), pltpu.SemaphoreType.DMA((3,))],
        compiler_params=pltpu.CompilerParams(vmem_limit_bytes=4 << 20),
    )(*[
        pltpu.with_memory_space_constraint(a, pltpu.HBM)
        for a in (views, partner.reshape(1, rows), weight.reshape(1, rows))
    ])
    oth = swap(own, "zl")
    far = exchange(spread, FAR)
    near = swap(far, "core")

    half, both, team = chunks * piece, 2 * rows, 2 * members
    flops = 2 * half * both * width
    score = pltpu.VMEM((2, BLOCK, both), f32)
    sums, ncol_far, nrow, e_far = call(
        functools.partial(far_kernel, sizes),
        [((2, 8, both), f32), ((half, width), bf16), ((both, width), bf16), ((half, both), f32)],
        (own, oth, far),
        [score],
        16,
        flops,
    )
    msg, ncol_near, e_near = call(
        functools.partial(near_kernel, sizes),
        [((team, 1, 3 * rows), f32), ((half, width), bf16), ((half, both), f32)],
        (own, oth, near, sums, nrow),
        [score],
        16,
        flops,
    )
    got = exchange(msg, TEAM)
    info, loss, cw = call(
        functools.partial(totals_kernel, sizes),
        [((4, rows), f32), ((1, rows), f32), ((2 * chunks, 1, 2 * piece), f32)],
        (oth, got, heft),
    )
    cw = exchange(cw, OWNERS)
    (grads,) = call(
        functools.partial(backward_kernel, sizes),
        [((team, piece, width), bf16)],
        (own, oth, ncol_far, ncol_near, e_far, e_near, info, cw),
        [pltpu.VMEM((2, half, both), bf16), pltpu.VMEM((width, both), f32)],
        16,
        2 * flops,
    )
    shares = exchange(grads, TEAM)
    (share,) = call(owner_kernel, [((members, piece, width), bf16)], (shares,))
    got = exchange(share, MP)
    grad, loss = pl.pallas_call(
        finish_kernel,
        name="finish",
        in_specs=[pl.BlockSpec(memory_space=pltpu.VMEM)] * 2,
        out_specs=[pl.BlockSpec(memory_space=pltpu.HBM)] * 2,
        out_shape=[
            jax.ShapeDtypeStruct((rows, width), f32),
            jax.ShapeDtypeStruct((1, rows), f32),
        ],
        scratch_shapes=[pltpu.VMEM((rows, width), f32), pltpu.SemaphoreType.DMA((members + 1,))],
        compiler_params=pltpu.CompilerParams(vmem_limit_bytes=4 << 20),
    )(got, loss)
    return loss.reshape(rows), grad


def solution(mesh):
    dims = {"zh": 4, "zl": 2, "yh": 4, "core": 2, "yl": 2, "x": 4}
    finer = Mesh(mesh.devices.reshape(tuple(dims.values())), tuple(dims))
    sizes = {**dims, "mp": dims["yl"] * dims["x"]}
    placed = (P(DP, None), P(DP), P(DP))
    return jax.shard_map(
        functools.partial(shards, sizes),
        mesh=finer,
        in_specs=placed,
        out_specs=(P(DP), P(DP, None)),
        check_vma=False,
    )
```
